128 devices in a mesh: space: 16 (over z_hi, x, core), chan: 8 (over y, z_lo).
Axes of the slice: x: 4, y: 4, z: 4 (z_hi: 2, z_lo: 2; z = z_hi * 2 + z_lo), core: 2. Of those that a mesh axis runs over, the one named last changes fastest.
Arguments:
- inputs: bfloat16 [128, 64, 32, 128], P('chan', 'space'), may hold values from -6 to 6
- filters: bfloat16 [27, 128, 128], P(None, 'chan'), may hold values from -0.109375 to 0.109375
- cotangent: bfloat16 [128, 64, 32, 128], P('chan', 'space'), may hold values from -6 to 6
Outputs:
- grad_inputs: bfloat16 [128, 64, 32, 128], P('chan', 'space')
- grad_filters: float32 [27, 128, 128], P(None, 'chan')
The draws below stay inside these ranges and needn't reach their ends.
All inputs are finite; a program needn't handle non-finite values.
Results may differ from the reference program's by a relative error of at most 0.0049.
Values may be sent and summed in bfloat16 or wider, within the bound.
A program may use at most 128 MiB of HBM per device.

```python
import math
import jax
import jax.numpy as jnp

C = 128
HEIGHT = 32
WIDTH = 128
DEPTH = 64
CELLS = 262144


def level_of(rng, shape, shards, least, top_value):
    gain, own = 1.0, jax.random.fold_in(rng, 6)
    for dim, parts in shards:
        draws = jnp.exp(jax.random.uniform(jax.random.fold_in(own, dim), (parts,), jnp.float32, least / len(shards), top_value / len(shards)))
        gain = gain * jnp.repeat(draws, shape[dim] // parts).reshape([-1 if axis == dim else 1 for axis in range(len(shape))])
    return gain


def bell_draw(own_key, dims, scale, bound, shards=(), held_as=jnp.bfloat16):
    result = scale * jax.random.normal(own_key, dims, jnp.float32)
    if shards:
        result = result * level_of(own_key, dims, shards, -0.22, 0.18)
    return jnp.clip(result, -bound, bound).astype(held_as)


def setup_inputs(seed: int = 0) -> dict:
    arg_keys = jax.random.split(jax.random.key(seed), 4)
    inputs = bell_draw(arg_keys[0], (C, DEPTH, HEIGHT, WIDTH), 1.0, 6.0, ((0, 8), (1, 16)))
    filters = bell_draw(arg_keys[1], (27, C, C), (27 * C) ** -0.5, 0.109375, ((1, 8),))
    cotangent = bell_draw(arg_keys[2], (C, DEPTH, HEIGHT, WIDTH), 1.0, 6.0, ((0, 8), (1, 16)))
    return dict(inputs=inputs, filters=filters, cotangent=cotangent)


def reference(inputs, filters, cotangent):
    plane_count = inputs.shape[1]
    row_count = inputs.shape[2]
    column_count = inputs.shape[3]
    padded_in = jnp.pad(inputs.astype(jnp.float32), ((0, 0), (1, 1), (1, 1), (1, 1)))
    weights32 = filters.astype(jnp.float32)
    pre_act = jnp.zeros((C, plane_count, row_count, column_count), jnp.float32)
    for offset in range(27):
        depth_off = offset // 9
        row_off = offset // 3 % 3
        column_off = offset % 3
        window = padded_in[:, depth_off:depth_off + plane_count, row_off:row_off + row_count, column_off:column_off + column_count]
        pre_act = pre_act + jnp.einsum('io,idhw->odhw', weights32[offset], window)
    sigma = jax.nn.sigmoid(pre_act)
    grad_out = (cotangent.astype(jnp.float32) * sigma * (1.0 + pre_act * (1.0 - sigma))).astype(jnp.bfloat16)
    grad32 = grad_out.astype(jnp.float32)
    grad_pad = jnp.pad(grad32, ((0, 0), (1, 1), (1, 1), (1, 1)))
    grad_in = jnp.zeros((C, plane_count, row_count, column_count), jnp.float32)
    pieces = []
    for offset in range(27):
        depth_off = offset // 9
        row_off = offset // 3 % 3
        column_off = offset % 3
        window = grad_pad[:, 2 - depth_off:2 - depth_off + plane_count, 2 - row_off:2 - row_off + row_count, 2 - column_off:2 - column_off + column_count]
        grad_in = grad_in + jnp.einsum('io,odhw->idhw', weights32[offset], window)
        source = padded_in[:, depth_off:depth_off + plane_count, row_off:row_off + row_count, column_off:column_off + column_count]
        pieces.append(jnp.einsum('idhw,odhw->io', source, grad32))
    grad_w = jnp.stack(pieces) * (1.0 / math.sqrt(CELLS))
    return (grad_in.astype(jnp.bfloat16), grad_w)
```

```python
import math

import jax
import jax.numpy as jnp
from jax import lax
from jax.experimental import pallas as pl
from jax.experimental.pallas import tpu as pltpu
from jax.sharding import PartitionSpec as P

MESH = pl.DeviceIdType.MESH
BF16 = jnp.bfloat16
F32 = jnp.float32
PITCH = 136


def row_block(c):
    y = lax.div(c, 2)
    z = lax.rem(c, 2)
    q = lax.rem(y, 2)
    return 2 * y + z + q - 2 * z * q


def remote(src, dst, send_sem, recv_sem, **where):
    return pltpu.make_async_remote_copy(
        src_ref=src, dst_ref=dst, send_sem=send_sem, recv_sem=recv_sem,
        device_id=where, device_id_type=MESH,
    )


def shift_lanes(block, by):
    lane = lax.broadcasted_iota(jnp.int32, (block.shape[0], 128), 1)
    edge = 0 if by == 1 else 127
    pieces = []
    for d in range(block.shape[1] // 128):
        rolled = pltpu.roll(block[:, 128 * d : 128 * d + 128], by % 128, 1)
        pieces.append(jnp.where(lane == edge, 0.0, rolled))
    return jnp.concatenate(pieces, axis=1)


def kernel(
    scale, x_ref, f_ref, t_ref, gi_ref, gw_ref,
    wide, xt, tt, ws, xb, ct, wg, wf, gb, gs, gw, gwb, abuf, sb, bbuf, cb, cbuf, gwf, gout, back,
    x_s, x_r, t_s, t_r, w_s, w_r, xh_s, xh_r, gh_s, gh_r, gi_s, gi_r,
    a_s, a_r, b_s, b_r, c_s, c_r, d_s, d_r,
):
    c = lax.axis_index("chan")
    g = lax.axis_index("space")
    r = row_block(c)
    core = lax.rem(g, 2)
    chip = lax.div(g, 2)
    mine = pl.ds(pl.multiple_of(16 * c, 16), 16)
    has_lo, has_hi = g > 0, g < 15
    has_up, has_down = r > 0, r < 7

    barrier = pltpu.get_barrier_semaphore()
    for k in range(1, 8):
        pl.semaphore_signal(barrier, inc=1, device_id={"chan": lax.rem(c + k, 8)}, device_id_type=MESH)
    for k in range(1, 16):
        pl.semaphore_signal(barrier, inc=1, device_id={"space": lax.rem(g + k, 16)}, device_id_type=MESH)
    for dg, has_g in ((-1, has_lo), (1, has_hi)):
        for dr, has_r in ((-1, has_up), (1, has_down)):
            both = jnp.logical_and(has_g, has_r)

            @pl.when(both)
            def _():
                pl.semaphore_signal(
                    barrier, inc=1,
                    device_id={"space": g + dg, "chan": row_block(r + dr)}, device_id_type=MESH,
                )

    xt[0] = jnp.zeros((16, 512), BF16)
    xt[33] = jnp.zeros((16, 512), BF16)

    @pl.when(g == 0)
    def _():
        xb[:, :, 0:128] = jnp.zeros((6, 128, 128), BF16)
        gb[:, :, 0:128] = jnp.zeros((6, 128, 128), BF16)

    @pl.when(g == 15)
    def _():
        xb[:, :, 640:768] = jnp.zeros((6, 128, 128), BF16)
        gb[:, :, 640:768] = jnp.zeros((6, 128, 128), BF16)

    @pl.when(r == 0)
    def _():
        gb[0] = jnp.zeros((128, 768), BF16)

    @pl.when(r == 7)
    def _():
        gb[5] = jnp.zeros((128, 768), BF16)

    for tap in range(27):
        a, b, cc = tap // 9, tap // 3 % 3, tap % 3
        at = 128 * (3 * (2 - a) + 2 - b)
        ws[cc, :, at : at + 128] = f_ref[tap]

    def to_rows(src, dst, first):
        for ch in range(16):
            wide[PITCH * ch : PITCH * ch + 128, :] = src[ch].reshape(128, 128).astype(F32)

        def step(h, _):
            for d in range(4):
                rows = wide[pl.ds(32 * d + h, 16, stride=PITCH), :]
                dst[first + h, :, 128 * d : 128 * d + 128] = rows.astype(BF16)
            return 0

        lax.fori_loop(0, 32, step, 0)

    to_rows(x_ref, xt, 1)

    sides_g = has_lo.astype(jnp.int32) + has_hi.astype(jnp.int32)
    sides_r = has_up.astype(jnp.int32) + has_down.astype(jnp.int32)
    pl.semaphore_wait(barrier, 22 + sides_g * sides_r)

    x_copies, w_copies, t_copies = [], [], []
    for k in range(1, 8):
        to = lax.rem(c + k, 8)
        x_copies.append(remote(
            xt.at[pl.ds(4 * row_block(to), 6)], xb.at[:, mine, 128:640],
            x_s.at[k - 1], x_r.at[k - 1], chan=to,
        ))
        x_copies[-1].start()
    for k in range(1, 8):
        to = lax.rem(c + k, 8)
        w_copies.append(remote(ws, wg.at[:, mine, :], w_s.at[k - 1], w_r.at[k - 1], chan=to))
        w_copies[-1].start()
    xb[:, mine, 128:640] = xt[pl.ds(4 * r, 6)]
    wg[:, mine, :] = ws[...]

    to_rows(t_ref, tt, 0)
    for k in range(1, 8):
        to = lax.rem(c + k, 8)
        t_copies.append(remote(
            tt.at[pl.ds(4 * row_block(to), 4)], ct.at[:, mine, :],
            t_s.at[k - 1], t_r.at[k - 1], chan=to,
        ))
        t_copies[-1].start()
    ct[:, mine, :] = tt[pl.ds(4 * r, 4)]

    for copy in x_copies:
        copy.wait_recv()
    lo_copy = remote(xb.at[:, :, 128:256], xb.at[:, :, 640:768], xh_s.at[0], xh_r.at[0], space=g - 1)
    hi_copy = remote(xb.at[:, :, 512:640], xb.at[:, :, 0:128], xh_s.at[1], xh_r.at[1], space=g + 1)
    pl.when(has_lo)(lambda: lo_copy.start())
    pl.when(has_hi)(lambda: hi_copy.start())

    for copy in w_copies:
        copy.wait_recv()
    for tap in range(27):
        a, b, cc = tap // 9, tap // 3 % 3, tap % 3
        at = 128 * (3 * (2 - a) + 2 - b)
        to = 128 * (3 * a + b)
        wf[128 * cc : 128 * cc + 128, to : to + 128] = wg[cc, :, at : at + 128].T

    pl.when(has_hi)(lambda: lo_copy.wait_recv())
    pl.when(has_lo)(lambda: hi_copy.wait_recv())
    for copy in t_copies:
        copy.wait_recv()

    def patches(src, h):
        rows = [src[h + b, :, 128 * a : 128 * a + 512] for a in range(3) for b in range(3)]
        return jnp.concatenate(rows, axis=0)

    def forward(h, _):
        acc = jnp.dot(wf[...], patches(xb, h), preferred_element_type=F32)
        pre = shift_lanes(acc[0:128], 1) + acc[128:256] + shift_lanes(acc[256:384], -1)
        sigma = 1.0 / (1.0 + jnp.exp(-pre))
        grad = ct[h].astype(F32) * sigma * (1.0 + pre * (1.0 - sigma))
        gb[h + 1, :, 128:640] = grad.astype(BF16)
        gs[h, 0:128, :] = shift_lanes(grad, -1).astype(BF16)
        gs[h, 128:256, :] = grad.astype(BF16)
        gs[h, 256:384, :] = shift_lanes(grad, 1).astype(BF16)
        return 0

    lax.fori_loop(0, 4, forward, 0)

    up, down = row_block(lax.max(r - 1, 0)), row_block(lax.min(r + 1, 7))
    rims = [
        (gb.at[1:5, :, 128:256], gb.at[1:5, :, 640:768], has_lo, has_hi, {"space": g - 1}),
        (gb.at[1:5, :, 512:640], gb.at[1:5, :, 0:128], has_hi, has_lo, {"space": g + 1}),
        (gb.at[1, :, 128:640], gb.at[5, :, 128:640], has_up, has_down, {"chan": up}),
        (gb.at[4, :, 128:640], gb.at[0, :, 128:640], has_down, has_up, {"chan": down}),
    ]
    for dg, plane, to_plane in ((-1, 128, 640), (1, 512, 0)):
        for dr, row, to_row in ((-1, 1, 5), (1, 4, 0)):
            has_g, from_g = (has_lo, has_hi) if dg < 0 else (has_hi, has_lo)
            has_r, from_r = (has_up, has_down) if dr < 0 else (has_down, has_up)
            rims.append((
                gb.at[row, :, plane : plane + 128], gb.at[to_row, :, to_plane : to_plane + 128],
                jnp.logical_and(has_g, has_r), jnp.logical_and(from_g, from_r),
                {"space": g + dg, "chan": up if dr < 0 else down},
            ))
    g_copies = []
    for n, (src, dst, sends, gets, where) in enumerate(rims):
        copy = remote(src, dst, gh_s.at[n], gh_r.at[n], **where)
        g_copies.append((copy, sends, gets))
        pl.when(sends)(copy.start)

    grads = jnp.concatenate([gs[h] for h in range(4)], axis=1)
    for tap in range(9):
        a, b = tap // 3, tap % 3
        rows = jnp.concatenate([xb[h + b, :, 128 * a : 128 * a + 512] for h in range(4)], axis=1)
        part = lax.dot_general(rows, grads, (((1,), (1,)), ((), ())), preferred_element_type=F32)
        for cc in range(3):
            gw[3 * tap + cc] = part[:, 128 * cc : 128 * cc + 128]
            gwb[3 * tap + cc] = part[:, 128 * cc : 128 * cc + 128].astype(BF16)
    for tap in range(27, 32):
        gw[tap] = jnp.zeros((128, 128), F32)
        gwb[tap] = jnp.zeros((128, 128), BF16)

    a_copy = remote(
        gwb.at[pl.ds(16 * (1 - core), 16)], abuf, a_s.at[0], a_r.at[0], space=g + 1 - 2 * core
    )
    a_copy.start()

    for copy, _, gets in g_copies:
        pl.when(gets)(copy.wait_recv)

    def backward(h, _):
        weights = jnp.concatenate([wg[cc] for cc in range(3)], axis=0)
        acc = jnp.dot(weights, patches(gb, h), preferred_element_type=F32)
        total = shift_lanes(acc[0:128], -1) + acc[128:256] + shift_lanes(acc[256:384], 1)
        gout[h] = total.astype(BF16)
        return 0

    gi_copies = []
    lax.fori_loop(0, 4, backward, 0)
    for k in range(1, 8):
        to = lax.rem(c + k, 8)
        gi_copies.append(remote(
            gout.at[:, pl.ds(pl.multiple_of(16 * to, 16), 16), :], back.at[pl.ds(4 * r, 4)],
            gi_s.at[k - 1], gi_r.at[k - 1], chan=to,
        ))
        gi_copies[-1].start()
    back[pl.ds(4 * r, 4)] = gout[:, mine, :]

    a_copy.wait_recv()
    sb[...] = (gw[pl.ds(16 * core, 16)] + abuf[...].astype(F32)).astype(BF16)
    b_copies = []
    for k in range(1, 8):
        to = lax.rem(c + k, 8)
        b_copies.append(remote(
            sb.at[:, pl.ds(pl.multiple_of(16 * to, 16), 16), :], bbuf.at[k - 1],
            b_s.at[k - 1], b_r.at[k - 1], chan=to,
        ))
        b_copies[-1].start()
    total = sb[:, mine, :].astype(F32)
    for k in range(7):
        b_copies[k].wait_recv()
        total = total + bbuf[k].astype(F32)
    cb[...] = total.astype(BF16)
    c_copies = []
    for k in range(1, 8):
        to = lax.rem(chip + k, 8)
        c_copies.append(remote(
            cb.at[pl.ds(2 * to, 2)], cbuf.at[k - 1], c_s.at[k - 1], c_r.at[k - 1],
            space=2 * to + core,
        ))
        c_copies[-1].start()
    total = cb[pl.ds(2 * chip, 2)].astype(F32)
    for k in range(7):
        c_copies[k].wait_recv()
        total = total + cbuf[k].astype(F32)
    piece = pl.ds(16 * core + 2 * chip, 2)
    gwf[piece] = total * scale
    d_copies = []
    for k in range(1, 16):
        d_copies.append(remote(
            gwf.at[piece], gwf.at[piece], d_s.at[k - 1], d_r.at[k - 1],
            space=lax.rem(g + k, 16),
        ))
        d_copies[-1].start()

    for copy in gi_copies:
        copy.wait_recv()
    for d in range(4):
        for h in range(32):
            wide[24 * h : 24 * h + 16, :] = back[h, :, 128 * d : 128 * d + 128].astype(F32)

        def step(ch, _):
            gi_ref[ch, d] = wide[pl.ds(ch, 32, stride=24), :].astype(BF16)
            return 0

        lax.fori_loop(0, 16, step, 0)

    for copy in d_copies:
        copy.wait_recv()
    gw_ref[...] = gwf[0:27]

    for copy in x_copies + w_copies + t_copies + gi_copies + b_copies + c_copies + d_copies:
        copy.wait_send()
    a_copy.wait_send()
    pl.when(has_lo)(lo_copy.wait_send)
    pl.when(has_hi)(hi_copy.wait_send)
    for copy, sends, _ in g_copies:
        pl.when(sends)(copy.wait_send)


def body(inputs, filters, cotangent):
    cells = inputs.shape[1] * lax.axis_size("space") * inputs.shape[2] * inputs.shape[3]
    scale = 1.0 / math.sqrt(cells)
    sems = [7, 7, 7, 7, 7, 7, 2, 2, 8, 8, 7, 7, 1, 1, 7, 7, 7, 7, 15, 15]
    scratch = [
        ((PITCH * 16, 128), F32),
        ((34, 16, 512), BF16),
        ((32, 16, 512), BF16),
        ((3, 16, 1152), BF16),
        ((6, 128, 768), BF16),
        ((4, 128, 512), BF16),
        ((3, 128, 1152), BF16),
        ((384, 1152), BF16),
        ((6, 128, 768), BF16),
        ((4, 384, 512), BF16),
        ((32, 128, 128), F32),
        ((32, 128, 128), BF16),
        ((16, 128, 128), BF16),
        ((16, 128, 128), BF16),
        ((7, 16, 16, 128), BF16),
        ((16, 16, 128), BF16),
        ((7, 2, 16, 128), BF16),
        ((32, 16, 128), F32),
        ((4, 128, 512), BF16),
        ((32, 16, 512), BF16),
    ]
    vmem = pl.BlockSpec(memory_space=pltpu.VMEM)
    return pl.pallas_call(
        lambda *refs: kernel(scale, *refs),
        out_shape=(
            jax.ShapeDtypeStruct(inputs.shape, BF16),
            jax.ShapeDtypeStruct(filters.shape, F32),
        ),
        in_specs=[vmem] * 3,
        out_specs=(vmem, vmem),
        scratch_shapes=[pltpu.VMEM(s, t) for s, t in scratch]
        + [pltpu.SemaphoreType.DMA((n,)) for n in sems],
        compiler_params=pltpu.CompilerParams(
            collective_id=0, has_side_effects=True, vmem_limit_bytes=60 * 2**20
        ),
        name="conv_backward",
    )(inputs, filters, cotangent)


def solution(mesh):
    placed = (P("chan", "space", None, None), P(None, "chan", None), P("chan", "space", None, None))
    return jax.shard_map(
        body,
        mesh=mesh,
        in_specs=placed,
        out_specs=(P("chan", "space", None, None), P(None, "chan", None)),
        check_vma=False,
    )
```

```python
import math

import jax
import jax.numpy as jnp
from jax import lax
from jax.experimental import pallas as pl
from jax.experimental.pallas import tpu as pltpu
from jax.sharding import PartitionSpec as P

MESH = pl.DeviceIdType.MESH
BF16 = jnp.bfloat16
F32 = jnp.float32
PITCH = 136


def row_block(c):
    y = lax.div(c, 2)
    z = lax.rem(c, 2)
    q = lax.rem(y, 2)
    return 2 * y + z + q - 2 * z * q


class Copy:
    def __init__(self, src, dst, send_sem, recv_sem, where, sends=None, gets=None):
        self.copy = pltpu.make_async_remote_copy(
            src_ref=src, dst_ref=dst, send_sem=send_sem, recv_sem=recv_sem,
            device_id=where, device_id_type=MESH,
        )
        self.sends, self.gets = sends, gets

    def start(self):
        self.copy.start() if self.sends is None else pl.when(self.sends)(self.copy.start)
        return self

    def wait_recv(self):
        self.copy.wait_recv() if self.gets is None else pl.when(self.gets)(self.copy.wait_recv)

    def wait_send(self):
        self.copy.wait_send() if self.sends is None else pl.when(self.sends)(self.copy.wait_send)


def shift_lanes(block, by):
    lane = lax.broadcasted_iota(jnp.int32, (block.shape[0], 128), 1)
    edge = 0 if by == 1 else 127
    pieces = []
    for d in range(block.shape[1] // 128):
        rolled = pltpu.roll(block[:, 128 * d : 128 * d + 128], by % 128, 1)
        pieces.append(jnp.where(lane == edge, 0.0, rolled))
    return jnp.concatenate(pieces, axis=1)


def kernel(
    scale, x_ref, f_ref, t_ref, gi_ref, gw_ref,
    wide, xt, tt, fp, xb, ct, wall, wg, wf, pre, gb, gs, gw, gwb, abuf, sb, xbuf, yb, ybuf, gwf,
    gout, back,
    x_s, x_r, t_s, t_r, wy_s, wy_r, wx_s, wx_r, wd_s, wd_r, xh_s, xh_r, gh_s, gh_r, gi_s, gi_r,
    a_s, a_r, b_s, b_r, y_s, y_r, d_s, d_r,
):
    c = lax.axis_index("chan")
    g = lax.axis_index("space")
    r = row_block(c)
    core = lax.rem(g, 2)
    px = lax.rem(lax.div(g, 2), 4)
    pz = lax.div(g, 8)
    sibling = g + 1 - 2 * core
    mine = pl.ds(pl.multiple_of(16 * c, 16), 16)
    has_lo, has_hi = g > 0, g < 15
    has_up, has_down = r > 0, r < 7

    def chan_peer(k):
        return lax.rem(c + k, 8)

    def x_peer(k):
        return 8 * pz + 2 * lax.rem(px + k, 4) + core

    barrier = pltpu.get_barrier_semaphore()
    for k in range(1, 8):
        pl.semaphore_signal(barrier, inc=1, device_id={"chan": chan_peer(k)}, device_id_type=MESH)
    for k in range(1, 16):
        pl.semaphore_signal(barrier, inc=1, device_id={"space": lax.rem(g + k, 16)}, device_id_type=MESH)
    for k in range(1, 8):
        pl.semaphore_signal(
            barrier, inc=1, device_id={"space": lax.rem(g + 8, 16), "chan": chan_peer(k)},
            device_id_type=MESH,
        )
    for dg, has_g in ((-1, has_lo), (1, has_hi)):
        for dr, has_r in ((-1, has_up), (1, has_down)):

            @pl.when(jnp.logical_and(has_g, has_r))
            def _():
                pl.semaphore_signal(
                    barrier, inc=1,
                    device_id={"space": g + dg, "chan": row_block(r + dr)}, device_id_type=MESH,
                )

    xt[0] = jnp.zeros((16, 512), BF16)
    xt[33] = jnp.zeros((16, 512), BF16)

    @pl.when(g == 0)
    def _():
        xb[:, :, 0:128] = jnp.zeros((6, 128, 128), BF16)
        gb[:, :, 0:128] = jnp.zeros((6, 128, 128), BF16)

    @pl.when(g == 15)
    def _():
        xb[:, :, 640:768] = jnp.zeros((6, 128, 128), BF16)
        gb[:, :, 640:768] = jnp.zeros((6, 128, 128), BF16)

    @pl.when(r == 0)
    def _():
        gb[0] = jnp.zeros((128, 768), BF16)

    @pl.when(r == 7)
    def _():
        gb[5] = jnp.zeros((128, 768), BF16)

    fp[0:27] = f_ref[...]
    fp[27:32] = jnp.zeros((5, 16, 128), BF16)

    def to_rows(src, dst, first):
        for ch in range(16):
            wide[PITCH * ch : PITCH * ch + 128, :] = src[ch].reshape(128, 128).astype(F32)

        def step(h, _):
            for d in range(4):
                rows = wide[pl.ds(32 * d + h, 16, stride=PITCH), :]
                dst[first + h, :, 128 * d : 128 * d + 128] = rows.astype(BF16)
            return 0

        lax.fori_loop(0, 32, step, 0)

    to_rows(x_ref, xt, 1)
    sides_g = has_lo.astype(jnp.int32) + has_hi.astype(jnp.int32)
    sides_r = has_up.astype(jnp.int32) + has_down.astype(jnp.int32)
    pl.semaphore_wait(barrier, 29 + sides_g * sides_r)

    part = 4 * (4 * core + px)
    wy_copies = [
        Copy(
            fp.at[pl.ds(part, 4)], wall.at[pl.ds(part, 4), mine, :],
            wy_s.at[k - 1], wy_r.at[k - 1], {"chan": chan_peer(k)},
        ).start()
        for k in range(1, 8)
    ]
    wall[pl.ds(part, 4), mine, :] = fp[pl.ds(part, 4)]
    x_copies = [
        Copy(
            xt.at[pl.ds(4 * row_block(chan_peer(k)), 6)], xb.at[:, mine, 128:640],
            x_s.at[k - 1], x_r.at[k - 1], {"chan": chan_peer(k)},
        ).start()
        for k in range(1, 8)
    ]
    xb[:, mine, 128:640] = xt[pl.ds(4 * r, 6)]
    to_rows(t_ref, tt, 0)
    t_copies = [
        Copy(
            tt.at[pl.ds(4 * row_block(chan_peer(k)), 4)], ct.at[:, mine, :],
            t_s.at[k - 1], t_r.at[k - 1], {"chan": chan_peer(k)},
        ).start()
        for k in range(1, 8)
    ]
    ct[:, mine, :] = tt[pl.ds(4 * r, 4)]
    for copy in wy_copies:
        copy.wait_recv()
    wx_copies = [
        Copy(
            wall.at[pl.ds(part, 4)], wall.at[pl.ds(part, 4)],
            wx_s.at[k - 1], wx_r.at[k - 1], {"space": x_peer(k)},
        ).start()
        for k in range(1, 4)
    ]
    wd_copies = []
    for k in range(4):
        if k:
            wx_copies[k - 1].wait_recv()
        piece = wall.at[pl.ds(4 * (4 * core + lax.rem(px + 4 - k, 4)), 4)]
        wd_copies.append(
            Copy(piece, piece, wd_s.at[k], wd_r.at[k], {"space": sibling}).start()
        )

    for copy in x_copies:
        copy.wait_recv()
    h_copies = [
        Copy(xb.at[:, :, 128:256], xb.at[:, :, 640:768], xh_s.at[0], xh_r.at[0],
             {"space": g - 1}, has_lo, has_hi).start(),
        Copy(xb.at[:, :, 512:640], xb.at[:, :, 0:128], xh_s.at[1], xh_r.at[1],
             {"space": g + 1}, has_hi, has_lo).start(),
    ]
    for copy in wd_copies:
        copy.wait_recv()
    for tap in range(27):
        a, b, cc = tap // 9, tap // 3 % 3, tap % 3
        block = wall[tap]
        rows = slice(128 * cc, 128 * cc + 128)
        wg[rows, 128 * (8 - 3 * a - b) : 128 * (9 - 3 * a - b)] = block
        wf[rows, 128 * (3 * a + b) : 128 * (3 * a + b + 1)] = block.T
    for copy in h_copies:
        copy.wait_recv()

    def patches(src, h):
        rows = [src[h + b, :, 128 * a : 128 * a + 512] for a in range(3) for b in range(3)]
        return jnp.concatenate(rows, axis=0)

    def forward(h, _):
        acc = jnp.dot(wf[...], patches(xb, h), preferred_element_type=F32)
        pre[h] = shift_lanes(acc[0:128], 1) + acc[128:256] + shift_lanes(acc[256:384], -1)
        return 0

    lax.fori_loop(0, 4, forward, 0)
    for copy in t_copies:
        copy.wait_recv()

    up, down = row_block(lax.max(r - 1, 0)), row_block(lax.min(r + 1, 7))
    row_rims, plane_rims = [], []

    def send_rims(row, to_row, has_r, from_r, to):
        n = 3 * len(row_rims)
        sent = [Copy(
            gb.at[row, :, 128:640], gb.at[to_row, :, 128:640], gh_s.at[n], gh_r.at[n],
            {"chan": to}, has_r, from_r,
        ).start()]
        for m, plane, to_plane, dg in ((1, 128, 640, -1), (2, 512, 0, 1)):
            has_g, from_g = (has_lo, has_hi) if dg < 0 else (has_hi, has_lo)
            sent.append(Copy(
                gb.at[row, :, plane : plane + 128], gb.at[to_row, :, to_plane : to_plane + 128],
                gh_s.at[n + m], gh_r.at[n + m], {"space": g + dg, "chan": to},
                jnp.logical_and(has_g, has_r), jnp.logical_and(from_g, from_r),
            ).start())
        row_rims.append(sent)

    for h in (0, 3, 1, 2):
        p = pre[h]
        sigma = 1.0 / (1.0 + jnp.exp(-p))
        grad = ct[h].astype(F32) * sigma * (1.0 + p * (1.0 - sigma))
        gb[h + 1, :, 128:640] = grad.astype(BF16)
        if h == 0:
            send_rims(1, 5, has_up, has_down, up)
        if h == 3:
            send_rims(4, 0, has_down, has_up, down)
        gs[h, 0:128, :] = shift_lanes(grad, -1).astype(BF16)
        gs[h, 128:256, :] = grad.astype(BF16)
        gs[h, 256:384, :] = shift_lanes(grad, 1).astype(BF16)
    plane_rims = [
        Copy(gb.at[1:5, :, 128:256], gb.at[1:5, :, 640:768], gh_s.at[6], gh_r.at[6],
             {"space": g - 1}, has_lo, has_hi).start(),
        Copy(gb.at[1:5, :, 512:640], gb.at[1:5, :, 0:128], gh_s.at[7], gh_r.at[7],
             {"space": g + 1}, has_hi, has_lo).start(),
    ]

    grads = jnp.concatenate([gs[h] for h in range(4)], axis=1)
    for tap in range(9):
        a, b = tap // 3, tap % 3
        rows = jnp.concatenate([xb[h + b, :, 128 * a : 128 * a + 512] for h in range(4)], axis=1)
        prod = lax.dot_general(rows, grads, (((1,), (1,)), ((), ())), preferred_element_type=F32)
        for cc in range(3):
            gw[3 * tap + cc] = prod[:, 128 * cc : 128 * cc + 128]
            gwb[3 * tap + cc] = prod[:, 128 * cc : 128 * cc + 128].astype(BF16)
    for tap in range(27, 32):
        gw[tap] = jnp.zeros((128, 128), F32)
        gwb[tap] = jnp.zeros((128, 128), BF16)

    a_copy = Copy(
        gwb.at[pl.ds(16 * (1 - core), 16)], abuf, a_s.at[0], a_r.at[0], {"space": sibling}
    ).start()

    gi_copies = []

    def backward(h):
        acc = jnp.dot(wg[...], patches(gb, h), preferred_element_type=F32)
        total = shift_lanes(acc[0:128], -1) + acc[128:256] + shift_lanes(acc[256:384], 1)
        gout[h] = total.astype(BF16)

    def send_rows(first, count, n):
        for k in range(1, 8):
            to = pl.ds(pl.multiple_of(16 * chan_peer(k), 16), 16)
            gi_copies.append(Copy(
                gout.at[pl.ds(first, count), to, :], back.at[pl.ds(4 * r + first, count)],
                gi_s.at[7 * n + k - 1], gi_r.at[7 * n + k - 1], {"chan": chan_peer(k)},
            ).start())
        back[pl.ds(4 * r + first, count)] = gout[first : first + count, mine, :]

    for copy in plane_rims:
        copy.wait_recv()
    backward(1)
    backward(2)
    send_rows(1, 2, 0)

    a_copy.wait_recv()
    sb[...] = (gw[pl.ds(16 * core, 16)] + abuf[...].astype(F32)).astype(BF16)
    b_copies = [
        Copy(
            sb.at[pl.ds(4 * lax.rem(px + k, 4), 4)], xbuf.at[k - 1], b_s.at[k - 1], b_r.at[k - 1],
            {"space": x_peer(k)},
        ).start()
        for k in range(1, 4)
    ]
    for sent in row_rims:
        for copy in sent:
            copy.wait_recv()
    backward(0)
    send_rows(0, 1, 1)
    backward(3)
    send_rows(3, 1, 2)

    total = sb[pl.ds(4 * px, 4)].astype(F32)
    for k in range(3):
        b_copies[k].wait_recv()
        total = total + xbuf[k].astype(F32)
    yb[...] = total.astype(BF16)
    y_copies = []
    for dz in range(2):
        for k in range(8):
            if dz or k:
                z, to = lax.rem(pz + dz, 2), chan_peer(k)
                n = 8 * dz + k - 1
                y_copies.append(Copy(
                    yb.at[pl.ds(2 * z, 2), pl.ds(pl.multiple_of(16 * to, 16), 16), :], ybuf.at[n],
                    y_s.at[n], y_r.at[n], {"space": 8 * z + 2 * px + core, "chan": to},
                ).start())
    total = yb[pl.ds(2 * pz, 2), mine, :].astype(F32)
    for n in range(15):
        y_copies[n].wait_recv()
        total = total + ybuf[n].astype(F32)
    piece = pl.ds(16 * core + 4 * px + 2 * pz, 2)
    gwf[piece] = total * scale
    d_copies = [
        Copy(
            gwf.at[piece], gwf.at[piece], d_s.at[k - 1], d_r.at[k - 1],
            {"space": lax.rem(g + k, 16)},
        ).start()
        for k in range(1, 16)
    ]
    for copy in gi_copies:
        copy.wait_recv()
    for d in range(4):
        for h in range(32):
            wide[24 * h : 24 * h + 16, :] = back[h, :, 128 * d : 128 * d + 128].astype(F32)

        def step(ch, _):
            gi_ref[ch, d] = wide[pl.ds(ch, 32, stride=24), :].astype(BF16)
            return 0

        lax.fori_loop(0, 16, step, 0)
    for copy in d_copies:
        copy.wait_recv()
    gw_ref[...] = gwf[0:27]

    copies = wy_copies + x_copies + t_copies + wx_copies + wd_copies + h_copies + row_rims[0]
    copies += row_rims[1] + plane_rims + [a_copy] + gi_copies + b_copies + y_copies + d_copies
    for copy in copies:
        copy.wait_send()


def body(inputs, filters, cotangent):
    cells = inputs.shape[1] * lax.axis_size("space") * inputs.shape[2] * inputs.shape[3]
    scale = 1.0 / math.sqrt(cells)
    pairs = [7, 7, 7, 3, 4, 2, 8, 21, 1, 3, 15, 15]
    scratch = [
        ((PITCH * 16, 128), F32),
        ((34, 16, 512), BF16),
        ((32, 16, 512), BF16),
        ((32, 16, 128), BF16),
        ((6, 128, 768), BF16),
        ((4, 128, 512), BF16),
        ((32, 128, 128), BF16),
        ((384, 1152), BF16),
        ((384, 1152), BF16),
        ((4, 128, 512), F32),
        ((6, 128, 768), BF16),
        ((4, 384, 512), BF16),
        ((32, 128, 128), F32),
        ((32, 128, 128), BF16),
        ((16, 128, 128), BF16),
        ((16, 128, 128), BF16),
        ((3, 4, 128, 128), BF16),
        ((4, 128, 128), BF16),
        ((15, 2, 16, 128), BF16),
        ((32, 16, 128), F32),
        ((4, 128, 512), BF16),
        ((32, 16, 512), BF16),
    ]
    vmem = pl.BlockSpec(memory_space=pltpu.VMEM)
    return pl.pallas_call(
        lambda *refs: kernel(scale, *refs),
        out_shape=(
            jax.ShapeDtypeStruct(inputs.shape, BF16),
            jax.ShapeDtypeStruct(filters.shape, F32),
        ),
        in_specs=[vmem] * 3,
        out_specs=(vmem, vmem),
        scratch_shapes=[pltpu.VMEM(s, t) for s, t in scratch]
        + [pltpu.SemaphoreType.DMA((n,)) for n in pairs for _ in range(2)],
        compiler_params=pltpu.CompilerParams(
            collective_id=0, has_side_effects=True, vmem_limit_bytes=60 * 2**20
        ),
        name="conv_backward",
    )(inputs, filters, cotangent)


def solution(mesh):
    placed = (P("chan", "space", None, None), P(None, "chan", None), P("chan", "space", None, None))
    return jax.shard_map(
        body,
        mesh=mesh,
        in_specs=placed,
        out_specs=(P("chan", "space", None, None), P(None, "chan", None)),
        check_vma=False,
    )
```

```python
import math

import jax
import jax.numpy as jnp
from jax import lax
from jax.experimental import pallas as pl
from jax.experimental.pallas import tpu as pltpu
from jax.sharding import PartitionSpec as P

MESH = pl.DeviceIdType.MESH
BF16 = jnp.bfloat16
F32 = jnp.float32
PITCH = 136
STEPS = (2, 1, 3, 0)


def row_block(c):
    y = lax.div(c, 2)
    z = lax.rem(c, 2)
    q = lax.rem(y, 2)
    return 2 * y + z + q - 2 * z * q


class Copy:
    def __init__(self, src, dst, send_sem, recv_sem, where, sends=None, gets=None):
        self.copy = pltpu.make_async_remote_copy(
            src_ref=src, dst_ref=dst, send_sem=send_sem, recv_sem=recv_sem,
            device_id=where, device_id_type=MESH,
        )
        self.sends, self.gets = sends, gets

    def start(self):
        self.copy.start() if self.sends is None else pl.when(self.sends)(self.copy.start)
        return self

    def wait_recv(self):
        self.copy.wait_recv() if self.gets is None else pl.when(self.gets)(self.copy.wait_recv)

    def wait_send(self):
        self.copy.wait_send() if self.sends is None else pl.when(self.sends)(self.copy.wait_send)


def shift_lanes(block, by):
    lane = lax.broadcasted_iota(jnp.int32, (block.shape[0], 128), 1)
    edge = 0 if by == 1 else 127
    pieces = []
    for d in range(block.shape[1] // 128):
        rolled = pltpu.roll(block[:, 128 * d : 128 * d + 128], by % 128, 1)
        pieces.append(jnp.where(lane == edge, 0.0, rolled))
    return jnp.concatenate(pieces, axis=1)


def kernel(
    scale, x_hbm, f_hbm, t_hbm, gi_hbm, gw_hbm,
    x_ref, f_ref, t_ref, gi_ref, gw_ref, wide, xt, tt, fp, xb, ct, wall, wg, wf, pre, gb, gs, gw, gwb, abuf, sb, xbuf, yb, ybuf, gwf,
    gout, back,
    x_s, x_r, t_s, t_r, wy_s, wy_r, wx_s, wx_r, wd_s, wd_r, xh_s, xh_r, gh_s, gh_r, gi_s, gi_r,
    a_s, a_r, b_s, b_r, y_s, y_r, d_s, d_r, io_sem,
):
    c = lax.axis_index("chan")
    g = lax.axis_index("space")
    r = row_block(c)
    core = lax.rem(g, 2)
    px = lax.rem(lax.div(g, 2), 4)
    pz = lax.div(g, 8)
    sibling = g + 1 - 2 * core
    mine = pl.ds(pl.multiple_of(16 * c, 16), 16)
    has_lo, has_hi = g > 0, g < 15
    has_up, has_down = r > 0, r < 7

    def chan_peer(k):
        return lax.rem(c + k, 8)

    def x_peer(k):
        return 8 * pz + 2 * lax.rem(px + k, 4) + core

    def half_peer(k):
        return 8 * pz + lax.rem(2 * px + core + k, 8)

    barrier = pltpu.get_barrier_semaphore()
    for k in range(1, 8):
        pl.semaphore_signal(barrier, inc=1, device_id={"chan": chan_peer(k)}, device_id_type=MESH)
    for k in range(1, 8):
        pl.semaphore_signal(barrier, inc=1, device_id={"space": half_peer(k)}, device_id_type=MESH)
    for k in range(8):
        pl.semaphore_signal(
            barrier, inc=1, device_id={"space": lax.rem(g + 8, 16), "chan": chan_peer(k)},
            device_id_type=MESH,
        )
    for edge, dg in ((7, 1), (8, -1)):

        @pl.when(g == edge)
        def _():
            pl.semaphore_signal(barrier, inc=1, device_id={"space": g + dg}, device_id_type=MESH)

    for dg, has_g in ((-1, has_lo), (1, has_hi)):
        for dr, has_r in ((-1, has_up), (1, has_down)):

            @pl.when(jnp.logical_and(has_g, has_r))
            def _():
                pl.semaphore_signal(
                    barrier, inc=1,
                    device_id={"space": g + dg, "chan": row_block(r + dr)}, device_id_type=MESH,
                )

    loads = [
        pltpu.make_async_copy(src, dst, io_sem.at[n])
        for n, (src, dst) in enumerate(((x_hbm, x_ref), (f_hbm, f_ref), (t_hbm, t_ref)))
    ]
    for load in loads:
        load.start()

    xt[0] = jnp.zeros((16, 512), BF16)
    xt[33] = jnp.zeros((16, 512), BF16)

    @pl.when(g == 0)
    def _():
        xb[:, :, 0:128] = jnp.zeros((6, 128, 128), BF16)
        gb[:, :, 0:128] = jnp.zeros((6, 128, 128), BF16)

    @pl.when(g == 15)
    def _():
        xb[:, :, 640:768] = jnp.zeros((6, 128, 128), BF16)
        gb[:, :, 640:768] = jnp.zeros((6, 128, 128), BF16)

    @pl.when(r == 0)
    def _():
        gb[0] = jnp.zeros((128, 768), BF16)

    @pl.when(r == 7)
    def _():
        gb[5] = jnp.zeros((128, 768), BF16)


    def to_rows(src, dst, first):
        for ch in range(16):
            wide[PITCH * ch : PITCH * ch + 128, :] = src[ch].reshape(128, 128).astype(F32)

        def step(h, _):
            for d in range(4):
                rows = wide[pl.ds(32 * d + h, 16, stride=PITCH), :]
                dst[first + h, :, 128 * d : 128 * d + 128] = rows.astype(BF16)
            return 0

        lax.fori_loop(0, 32, step, 0)

    loads[0].wait()
    to_rows(x_ref, xt, 1)
    sides_g = has_lo.astype(jnp.int32) + has_hi.astype(jnp.int32)
    sides_r = has_up.astype(jnp.int32) + has_down.astype(jnp.int32)
    middle = (g == 7).astype(jnp.int32) + (g == 8).astype(jnp.int32)
    loads[1].wait()
    fp[0:27] = f_ref[...]
    fp[27:32] = jnp.zeros((5, 16, 128), BF16)
    pl.semaphore_wait(barrier, 22 + middle + sides_g * sides_r)

    part = 4 * (4 * core + px)
    some = part < 28
    wy_copies = [
        Copy(
            fp.at[pl.ds(part, 4)], wall.at[pl.ds(part, 4), mine, :],
            wy_s.at[k - 1], wy_r.at[k - 1], {"chan": chan_peer(k)}, some, some,
        ).start()
        for k in range(1, 8)
    ]
    wall[pl.ds(part, 4), mine, :] = fp[pl.ds(part, 4)]
    x_copies = [
        Copy(
            xt.at[pl.ds(4 * row_block(chan_peer(k)), 6)], xb.at[:, mine, 128:640],
            x_s.at[k - 1], x_r.at[k - 1], {"chan": chan_peer(k)},
        ).start()
        for k in range(1, 8)
    ]
    xb[:, mine, 128:640] = xt[pl.ds(4 * r, 6)]
    loads[2].wait()
    to_rows(t_ref, tt, 0)
    t_copies = [
        Copy(
            tt.at[pl.ds(4 * row_block(chan_peer(k)), 4)], ct.at[:, mine, :],
            t_s.at[k - 1], t_r.at[k - 1], {"chan": chan_peer(k)},
        ).start()
        for k in range(1, 8)
    ]
    ct[:, mine, :] = tt[pl.ds(4 * r, 4)]
    for copy in wy_copies:
        copy.wait_recv()
    wx_copies = [
        Copy(
            wall.at[pl.ds(part, 4)], wall.at[pl.ds(part, 4)],
            wx_s.at[k - 1], wx_r.at[k - 1], {"space": x_peer(k)},
            some, core + lax.rem(px + 4 - k, 4) < 4,
        ).start()
        for k in range(1, 4)
    ]

    for copy in x_copies:
        copy.wait_recv()
    h_copies = [
        Copy(xb.at[:, :, 128:256], xb.at[:, :, 640:768], xh_s.at[0], xh_r.at[0],
             {"space": g - 1}, has_lo, has_hi).start(),
        Copy(xb.at[:, :, 512:640], xb.at[:, :, 0:128], xh_s.at[1], xh_r.at[1],
             {"space": g + 1}, has_hi, has_lo).start(),
    ]
    wd_copies = []
    for k in range(4):
        if k:
            wx_copies[k - 1].wait_recv()
        owner = lax.rem(px + 4 - k, 4)
        piece = wall.at[pl.ds(4 * (4 * core + owner), 4)]
        wd_copies.append(Copy(
            piece, piece, wd_s.at[k], wd_r.at[k], {"space": sibling},
            core + owner < 4, 1 - core + owner < 4,
        ).start())
    for copy in wd_copies:
        copy.wait_recv()
    for tap in range(27):
        a, b, cc = tap // 9, tap // 3 % 3, tap % 3
        block = wall[tap]
        rows = slice(128 * cc, 128 * cc + 128)
        wg[rows, 128 * (8 - 3 * a - b) : 128 * (9 - 3 * a - b)] = block
        wf[rows, 128 * (3 * a + b) : 128 * (3 * a + b + 1)] = block.T
    for copy in h_copies:
        copy.wait_recv()

    def patches(src, h):
        rows = [src[h + b, :, 128 * a : 128 * a + 512] for a in range(3) for b in range(3)]
        return jnp.concatenate(rows, axis=0)

    def forward(h, _):
        acc = jnp.dot(wf[...], patches(xb, h), preferred_element_type=F32)
        pre[h] = shift_lanes(acc[0:128], 1) + acc[128:256] + shift_lanes(acc[256:384], -1)
        return 0

    lax.fori_loop(0, 4, forward, 0)
    for copy in t_copies:
        copy.wait_recv()

    up, down = row_block(lax.max(r - 1, 0)), row_block(lax.min(r + 1, 7))
    row_rims, plane_rims = [], []

    def send_rims(row, to_row, has_r, from_r, to):
        n = 3 * len(row_rims)
        sent = [Copy(
            gb.at[row, :, 128:640], gb.at[to_row, :, 128:640], gh_s.at[n], gh_r.at[n],
            {"chan": to}, has_r, from_r,
        ).start()]
        for m, plane, to_plane, dg in ((1, 128, 640, -1), (2, 512, 0, 1)):
            has_g, from_g = (has_lo, has_hi) if dg < 0 else (has_hi, has_lo)
            sent.append(Copy(
                gb.at[row, :, plane : plane + 128], gb.at[to_row, :, to_plane : to_plane + 128],
                gh_s.at[n + m], gh_r.at[n + m], {"space": g + dg, "chan": to},
                jnp.logical_and(has_g, has_r), jnp.logical_and(from_g, from_r),
            ).start())
        row_rims.append(sent)

    for h in (0, 3, 1, 2):
        p = pre[h]
        sigma = 1.0 / (1.0 + jnp.exp(-p))
        grad = ct[h].astype(F32) * sigma * (1.0 + p * (1.0 - sigma))
        gb[h + 1, :, 128:640] = grad.astype(BF16)
        if h == 0:
            send_rims(1, 5, has_up, has_down, up)
        if h == 3:
            send_rims(4, 0, has_down, has_up, down)
        gs[h, 0:128, :] = shift_lanes(grad, -1).astype(BF16)
        gs[h, 128:256, :] = grad.astype(BF16)
        gs[h, 256:384, :] = shift_lanes(grad, 1).astype(BF16)
    plane_rims = [
        Copy(gb.at[1:5, :, 128:256], gb.at[1:5, :, 640:768], gh_s.at[6], gh_r.at[6],
             {"space": g - 1}, has_lo, has_hi).start(),
        Copy(gb.at[1:5, :, 512:640], gb.at[1:5, :, 0:128], gh_s.at[7], gh_r.at[7],
             {"space": g + 1}, has_hi, has_lo).start(),
    ]

    grads = jnp.concatenate([gs[h] for h in range(4)], axis=1)

    def product(ab):
        lanes = pl.ds(pl.multiple_of(128 * lax.div(ab, 3), 128), 512)
        rows = jnp.concatenate([xb[h + lax.rem(ab, 3), :, lanes] for h in range(4)], axis=1)
        return lax.dot_general(rows, grads, (((1,), (1,)), ((), ())), preferred_element_type=F32)

    ninth = product(jnp.int32(8))
    for n in range(8):
        last = ninth[:, 128 * n : 128 * n + 128] if n < 3 else jnp.zeros((128, 128), F32)
        gw[n, 3] = last
        gwb[n, 3] = last.astype(BF16)
    a_copies, b_copies = [], []

    def pair_sum(j):
        a_copies[j].wait_recv()
        q = lax.rem(px + STEPS[j], 4)
        total = gw[4 * core + q] + abuf[j].astype(F32)
        if STEPS[j] == 0:
            return total
        sb[j] = total.astype(BF16)
        b_copies.append(Copy(
            sb.at[j], xbuf.at[j], b_s.at[j], b_r.at[j], {"space": x_peer(STEPS[j])}
        ).start())

    for j in range(4):
        q = lax.rem(px + STEPS[j], 4)
        other, own = 4 * (1 - core) + q, 4 * core + q
        prod = product(other)
        for cc in range(3):
            gwb[other, cc] = prod[:, 128 * cc : 128 * cc + 128].astype(BF16)
        a_copies.append(Copy(
            gwb.at[other], abuf.at[j], a_s.at[j], a_r.at[j], {"space": sibling}
        ).start())
        prod = product(own)
        for cc in range(3):
            gw[own, cc] = prod[:, 128 * cc : 128 * cc + 128]
        if j:
            pair_sum(j - 1)

    gi_copies = []

    def backward(h):
        acc = jnp.dot(wg[...], patches(gb, h), preferred_element_type=F32)
        total = shift_lanes(acc[0:128], -1) + acc[128:256] + shift_lanes(acc[256:384], 1)
        gout[h] = total.astype(BF16)

    def send_rows(first, count, n):
        for k in range(1, 8):
            to = pl.ds(pl.multiple_of(16 * chan_peer(k), 16), 16)
            gi_copies.append(Copy(
                gout.at[pl.ds(first, count), to, :], back.at[pl.ds(4 * r + first, count)],
                gi_s.at[7 * n + k - 1], gi_r.at[7 * n + k - 1], {"chan": chan_peer(k)},
            ).start())
        back[pl.ds(4 * r + first, count)] = gout[first : first + count, mine, :]

    for copy in plane_rims:
        copy.wait_recv()
    backward(1)
    backward(2)
    send_rows(1, 2, 0)

    for sent in row_rims:
        for copy in sent:
            copy.wait_recv()
    backward(0)
    send_rows(0, 1, 1)
    backward(3)
    send_rows(3, 1, 2)

    total = pair_sum(3)
    for j in range(3):
        b_copies[j].wait_recv()
        total = total + xbuf[j].astype(F32)
    yb[...] = total.astype(BF16)
    y_copies = []
    for dz in range(2):
        for k in range(8):
            if dz or k:
                z, to = lax.rem(pz + dz, 2), chan_peer(k)
                n = 8 * dz + k - 1
                y_copies.append(Copy(
                    yb.at[:, pl.ds(pl.multiple_of(16 * to, 16), 16), :], ybuf.at[8 * pz + c],
                    y_s.at[n], y_r.at[n], {"space": 8 * z + 2 * px + core, "chan": to},
                ).start())
    ybuf[8 * pz + c] = yb[:, mine, :]
    for copy in y_copies:
        copy.wait_recv()
    total = ybuf[0].astype(F32)
    for n in range(1, 16):
        total = total + ybuf[n].astype(F32)
    piece = gwf.at[4 * core + px]
    piece[...] = total.astype(BF16)
    d_copies = [
        Copy(piece, piece, d_s.at[k - 1], d_r.at[k - 1], {"space": half_peer(k)}).start()
        for k in range(1, 8)
    ]
    for copy in gi_copies:
        copy.wait_recv()
    for d in range(4):
        for h in range(32):
            wide[24 * h : 24 * h + 16, :] = back[h, :, 128 * d : 128 * d + 128].astype(F32)

        def step(ch, _):
            gi_ref[ch, d] = wide[pl.ds(ch, 32, stride=24), :].astype(BF16)
            return 0

        lax.fori_loop(0, 16, step, 0)
    out = pltpu.make_async_copy(gi_ref, gi_hbm, io_sem.at[0])
    out.start()
    for copy in d_copies:
        copy.wait_recv()
    for tap in range(27):
        n, slot = (tap // 3, tap % 3) if tap < 24 else (tap - 24, 3)
        gw_ref[tap] = gwf[n, slot].astype(F32) * scale
    out_w = pltpu.make_async_copy(gw_ref, gw_hbm, io_sem.at[1])
    out_w.start()

    copies = wy_copies + x_copies + t_copies + wx_copies + wd_copies + h_copies + row_rims[0]
    copies += row_rims[1] + plane_rims + a_copies + gi_copies + b_copies + y_copies + d_copies
    for copy in copies:
        copy.wait_send()
    out.wait()
    out_w.wait()


def body(inputs, filters, cotangent):
    cells = inputs.shape[1] * lax.axis_size("space") * inputs.shape[2] * inputs.shape[3]
    scale = 1.0 / math.sqrt(cells)
    pairs = [7, 7, 7, 3, 4, 2, 8, 21, 4, 3, 15, 7]
    scratch = [
        (inputs.shape, BF16),
        (filters.shape, BF16),
        (inputs.shape, BF16),
        (inputs.shape, BF16),
        (filters.shape, F32),
        ((PITCH * 16, 128), F32),
        ((34, 16, 512), BF16),
        ((32, 16, 512), BF16),
        ((32, 16, 128), BF16),
        ((6, 128, 768), BF16),
        ((4, 128, 512), BF16),
        ((32, 128, 128), BF16),
        ((384, 1152), BF16),
        ((384, 1152), BF16),
        ((4, 128, 512), F32),
        ((6, 128, 768), BF16),
        ((4, 384, 512), BF16),
        ((8, 4, 128, 128), F32),
        ((8, 4, 128, 128), BF16),
        ((4, 4, 128, 128), BF16),
        ((3, 4, 128, 128), BF16),
        ((3, 4, 128, 128), BF16),
        ((4, 128, 128), BF16),
        ((16, 4, 16, 128), BF16),
        ((8, 4, 16, 128), BF16),
        ((4, 128, 512), BF16),
        ((32, 16, 512), BF16),
    ]
    hbm = pl.BlockSpec(memory_space=pl.ANY)
    return pl.pallas_call(
        lambda *refs: kernel(scale, *refs),
        out_shape=(
            jax.ShapeDtypeStruct(inputs.shape, BF16),
            jax.ShapeDtypeStruct(filters.shape, F32),
        ),
        in_specs=[hbm] * 3,
        out_specs=(hbm, hbm),
        scratch_shapes=[pltpu.VMEM(s, t) for s, t in scratch]
        + [pltpu.SemaphoreType.DMA((n,)) for n in pairs for _ in range(2)]
        + [pltpu.SemaphoreType.DMA((3,))],
        compiler_params=pltpu.CompilerParams(
            collective_id=0, has_side_effects=True, vmem_limit_bytes=60 * 2**20
        ),
        name="conv_backward",
    )(inputs, filters, cotangent)


def solution(mesh):
    placed = (P("chan", "space", None, None), P(None, "chan", None), P("chan", "space", None, None))
    return jax.shard_map(
        body,
        mesh=mesh,
        in_specs=placed,
        out_specs=(P("chan", "space", None, None), P(None, "chan", None)),
        check_vma=False,
    )
```

```python
import math

import jax
import jax.numpy as jnp
from jax import lax
from jax.experimental import pallas as pl
from jax.experimental.pallas import tpu as pltpu
from jax.sharding import PartitionSpec as P

MESH = pl.DeviceIdType.MESH
BF16 = jnp.bfloat16
F32 = jnp.float32
PITCH = 136
STEPS = (2, 1, 3, 0)


def row_block(c):
    y = lax.div(c, 2)
    z = lax.rem(c, 2)
    q = lax.rem(y, 2)
    return 2 * y + z + q - 2 * z * q


class Copy:
    def __init__(self, src, dst, send_sem, recv_sem, where, sends=None, gets=None):
        self.copy = pltpu.make_async_remote_copy(
            src_ref=src, dst_ref=dst, send_sem=send_sem, recv_sem=recv_sem,
            device_id=where, device_id_type=MESH,
        )
        self.sends, self.gets = sends, gets

    def start(self):
        self.copy.start() if self.sends is None else pl.when(self.sends)(self.copy.start)
        return self

    def wait_recv(self):
        self.copy.wait_recv() if self.gets is None else pl.when(self.gets)(self.copy.wait_recv)

    def wait_send(self):
        self.copy.wait_send() if self.sends is None else pl.when(self.sends)(self.copy.wait_send)


def drain(like, sem, when=None):
    wait = pltpu.make_async_copy(like, like, sem).wait
    wait() if when is None else pl.when(when)(wait)


def shift_lanes(block, by):
    lane = lax.broadcasted_iota(jnp.int32, (block.shape[0], 128), 1)
    edge = 0 if by == 1 else 127
    pieces = []
    for d in range(block.shape[1] // 128):
        rolled = pltpu.roll(block[:, 128 * d : 128 * d + 128], by % 128, 1)
        pieces.append(jnp.where(lane == edge, 0.0, rolled))
    return jnp.concatenate(pieces, axis=1)


def kernel(
    scale, x_hbm, f_hbm, t_hbm, gi_hbm, gw_hbm,
    x_ref, f_ref, t_ref, gi_ref, gw_ref, wide, xt, tt, fp, xb, ct, wall, wg, wf, pre, gb, gs, gw, gwb, abuf, sb, xbuf,
    gw9, gwb9, abuf9, sb9, xbuf9, yb, ybuf, gwf,
    gout, back,
    x_s, x_r, t_s, t_r, wy_s, wy_r, wx_s, wx_r, wd_s, wd_r, xh_s, xh_r, gh_s, gh_r, gi_s, gi_r,
    a_s, a_r, a9_s, a9_r, b_s, b_r, b9_s, b9_r, y_s, y_r, d_s, d_r, io_sem,
):
    c = lax.axis_index("chan")
    g = lax.axis_index("space")
    r = row_block(c)
    core = lax.rem(g, 2)
    px = lax.rem(lax.div(g, 2), 4)
    pz = lax.div(g, 8)
    sibling = g + 1 - 2 * core
    mine = pl.ds(pl.multiple_of(16 * c, 16), 16)
    has_lo, has_hi = g > 0, g < 15
    has_up, has_down = r > 0, r < 7

    def chan_peer(k):
        return lax.rem(c + k, 8)

    def x_peer(k):
        return 8 * pz + 2 * lax.rem(px + k, 4) + core

    def half_peer(k):
        return 8 * pz + lax.rem(2 * px + core + k, 8)

    barrier = pltpu.get_barrier_semaphore()
    for k in range(1, 8):
        pl.semaphore_signal(barrier, inc=1, device_id={"chan": chan_peer(k)}, device_id_type=MESH)
    for k in range(1, 8):
        pl.semaphore_signal(barrier, inc=1, device_id={"space": half_peer(k)}, device_id_type=MESH)
    for k in range(8):
        pl.semaphore_signal(
            barrier, inc=1, device_id={"space": lax.rem(g + 8, 16), "chan": chan_peer(k)},
            device_id_type=MESH,
        )
    for edge, dg in ((7, 1), (8, -1)):

        @pl.when(g == edge)
        def _():
            pl.semaphore_signal(barrier, inc=1, device_id={"space": g + dg}, device_id_type=MESH)

    for dg, has_g in ((-1, has_lo), (1, has_hi)):
        for dr, has_r in ((-1, has_up), (1, has_down)):

            @pl.when(jnp.logical_and(has_g, has_r))
            def _():
                pl.semaphore_signal(
                    barrier, inc=1,
                    device_id={"space": g + dg, "chan": row_block(r + dr)}, device_id_type=MESH,
                )

    loads = [
        pltpu.make_async_copy(src, dst, io_sem.at[n])
        for n, (src, dst) in enumerate(((x_hbm, x_ref), (f_hbm, f_ref), (t_hbm, t_ref)))
    ]
    for load in loads:
        load.start()

    xt[0] = jnp.zeros((16, 512), BF16)
    xt[33] = jnp.zeros((16, 512), BF16)

    @pl.when(g == 0)
    def _():
        xb[:, :, 0:128] = jnp.zeros((6, 128, 128), BF16)
        gb[:, :, 0:128] = jnp.zeros((6, 128, 128), BF16)

    @pl.when(g == 15)
    def _():
        xb[:, :, 640:768] = jnp.zeros((6, 128, 128), BF16)
        gb[:, :, 640:768] = jnp.zeros((6, 128, 128), BF16)

    @pl.when(r == 0)
    def _():
        gb[0] = jnp.zeros((128, 768), BF16)

    @pl.when(r == 7)
    def _():
        gb[5] = jnp.zeros((128, 768), BF16)


    def to_rows(src, dst, first):
        for ch in range(16):
            wide[PITCH * ch : PITCH * ch + 128, :] = src[ch].reshape(128, 128).astype(F32)

        def step(h, _):
            for d in range(4):
                rows = wide[pl.ds(32 * d + h, 16, stride=PITCH), :]
                dst[first + h, :, 128 * d : 128 * d + 128] = rows.astype(BF16)
            return 0

        lax.fori_loop(0, 32, step, 0)

    loads[0].wait()
    to_rows(x_ref, xt, 1)
    sides_g = has_lo.astype(jnp.int32) + has_hi.astype(jnp.int32)
    sides_r = has_up.astype(jnp.int32) + has_down.astype(jnp.int32)
    middle = (g == 7).astype(jnp.int32) + (g == 8).astype(jnp.int32)
    loads[1].wait()
    fp[0:27] = f_ref[...]
    fp[27:32] = jnp.zeros((5, 16, 128), BF16)
    pl.semaphore_wait(barrier, 22 + middle + sides_g * sides_r)

    part = 4 * (4 * core + px)
    some = part < 28
    wy_copies = [
        Copy(
            fp.at[pl.ds(part, 4)], wall.at[pl.ds(part, 4), mine, :],
            wy_s, wy_r, {"chan": chan_peer(k)}, some, some,
        ).start()
        for k in range(1, 8)
    ]
    wall[pl.ds(part, 4), mine, :] = fp[pl.ds(part, 4)]
    x_copies = [
        Copy(
            xt.at[pl.ds(4 * row_block(chan_peer(k)), 6)], xb.at[:, mine, 128:640],
            x_s, x_r.at[k - 1], {"chan": chan_peer(k)},
        ).start()
        for k in range(1, 8)
    ]
    xb[:, mine, 128:640] = xt[pl.ds(4 * r, 6)]
    loads[2].wait()
    to_rows(t_ref, tt, 0)
    t_copies = [
        Copy(
            tt.at[pl.ds(4 * row_block(chan_peer(k)), 4)], ct.at[:, mine, :],
            t_s, t_r, {"chan": chan_peer(k)},
        ).start()
        for k in range(1, 8)
    ]
    ct[:, mine, :] = tt[pl.ds(4 * r, 4)]
    drain(fp.at[0:28], wy_r, some)
    wx_copies = [
        Copy(
            wall.at[pl.ds(part, 4)], wall.at[pl.ds(part, 4)],
            wx_s, wx_r.at[k - 1], {"space": x_peer(k)},
            some, core + lax.rem(px + 4 - k, 4) < 4,
        ).start()
        for k in range(1, 4)
    ]

    wd_copies = []

    def pass_filters(k):
        owner = lax.rem(px + 4 - k, 4)
        piece = wall.at[pl.ds(4 * (4 * core + owner), 4)]
        wd_copies.append(Copy(
            piece, piece, wd_s, wd_r, {"space": sibling},
            core + owner < 4, 1 - core + owner < 4,
        ).start())

    pass_filters(0)

    h_copies = []

    def pass_rims(k):
        rows = pl.ds(pl.multiple_of(16 * lax.rem(c + 8 - k, 8), 16), 16)
        for n, at, to, dg in ((0, 128, 640, -1), (1, 512, 0, 1)):
            has_g, from_g = (has_lo, has_hi) if dg < 0 else (has_hi, has_lo)
            h_copies.append(Copy(
                xb.at[:, rows, at : at + 128], xb.at[:, rows, to : to + 128],
                xh_s.at[n], xh_r.at[n], {"space": g + dg}, has_g, from_g,
            ).start())

    pass_rims(0)
    for k in range(1, 6):
        x_copies[k - 1].wait_recv()
        pass_rims(k)
    for k in range(1, 4):
        wx_copies[k - 1].wait_recv()
        pass_filters(k)
    for k in range(6, 8):
        x_copies[k - 1].wait_recv()
        pass_rims(k)
    drain(wall.at[0:12], wd_r, core == 0)
    drain(wall.at[0:16], wd_r, core == 1)
    for tap in range(27):
        a, b, cc = tap // 9, tap // 3 % 3, tap % 3
        block = wall[tap]
        rows = slice(128 * cc, 128 * cc + 128)
        wg[rows, 128 * (8 - 3 * a - b) : 128 * (9 - 3 * a - b)] = block
        wf[rows, 128 * (3 * a + b) : 128 * (3 * a + b + 1)] = block.T
    drain(xb.at[:, :, 640:768], xh_r.at[0], has_hi)
    drain(xb.at[:, :, 0:128], xh_r.at[1], has_lo)

    def patches(src, h):
        rows = [src[h + b, :, 128 * a : 128 * a + 512] for a in range(3) for b in range(3)]
        return jnp.concatenate(rows, axis=0)

    def forward(h, _):
        acc = jnp.dot(wf[...], patches(xb, h), preferred_element_type=F32)
        pre[h] = shift_lanes(acc[0:128], 1) + acc[128:256] + shift_lanes(acc[256:384], -1)
        return 0

    lax.fori_loop(0, 4, forward, 0)
    drain(ct.at[:, 0:112, :], t_r)

    up, down = row_block(lax.max(r - 1, 0)), row_block(lax.min(r + 1, 7))
    row_rims, plane_rims = [], []

    def send_rims(row, to_row, has_r, from_r, to):
        n = 3 * len(row_rims)
        sent = [Copy(
            gb.at[row, :, 128:640], gb.at[to_row, :, 128:640], gh_s.at[n], gh_r.at[n],
            {"chan": to}, has_r, from_r,
        ).start()]
        for m, plane, to_plane, dg in ((1, 128, 640, -1), (2, 512, 0, 1)):
            has_g, from_g = (has_lo, has_hi) if dg < 0 else (has_hi, has_lo)
            sent.append(Copy(
                gb.at[row, :, plane : plane + 128], gb.at[to_row, :, to_plane : to_plane + 128],
                gh_s.at[n + m], gh_r.at[n + m], {"space": g + dg, "chan": to},
                jnp.logical_and(has_g, has_r), jnp.logical_and(from_g, from_r),
            ).start())
        row_rims.append(sent)

    for h in (0, 3, 1, 2):
        p = pre[h]
        sigma = 1.0 / (1.0 + jnp.exp(-p))
        grad = ct[h].astype(F32) * sigma * (1.0 + p * (1.0 - sigma))
        gb[h + 1, :, 128:640] = grad.astype(BF16)
        for n, at, to, dg in ((6, 128, 640, -1), (7, 512, 0, 1)):
            has_g, from_g = (has_lo, has_hi) if dg < 0 else (has_hi, has_lo)
            plane_rims.append(Copy(
                gb.at[h + 1, :, at : at + 128], gb.at[h + 1, :, to : to + 128],
                gh_s.at[n], gh_r.at[n], {"space": g + dg}, has_g, from_g,
            ).start())
        if h == 0:
            send_rims(1, 5, has_up, has_down, up)
        if h == 3:
            send_rims(4, 0, has_down, has_up, down)
        gs[h, 0:128, :] = shift_lanes(grad, -1).astype(BF16)
        gs[h, 128:256, :] = grad.astype(BF16)
        gs[h, 256:384, :] = shift_lanes(grad, 1).astype(BF16)

    grads = jnp.concatenate([gs[h] for h in range(4)], axis=1)

    def product(*offsets):
        sides = []
        for ab in offsets:
            lanes = pl.ds(pl.multiple_of(128 * lax.div(ab, 3), 128), 512)
            rows = [xb[h + lax.rem(ab, 3), :, lanes] for h in range(4)]
            sides.append(jnp.concatenate(rows, axis=1))
        side = sides[0] if len(sides) == 1 else jnp.concatenate(sides, axis=0)
        return lax.dot_general(grads, side, (((1,), (1,)), ((), ())), preferred_element_type=F32)

    a_copies, b_copies = [], []

    def pair_sum(j):
        a_copies[j].wait_recv()
        q = lax.rem(px + STEPS[j], 4)
        total = gw[4 * core + q] + abuf[j].astype(F32)
        if STEPS[j] == 0:
            return total
        sb[j] = total.astype(BF16)
        b_copies.append(Copy(
            sb.at[j], xbuf.at[j], b_s, b_r, {"space": x_peer(STEPS[j])}
        ).start())

    for j in range(4):
        q = lax.rem(px + STEPS[j], 4)
        prod = product(q, q + 4)
        for cc in range(3):
            for n in range(2):
                block = prod[128 * cc : 128 * cc + 128, 128 * n : 128 * n + 128]
                gw[4 * n + q, cc] = block
                gwb[4 * n + q, cc] = block.astype(BF16)
        a_copies.append(Copy(
            gwb.at[4 * (1 - core) + q], abuf.at[j], a_s, a_r.at[j], {"space": sibling}
        ).start())
        if j:
            pair_sum(j - 1)
    ninth = product(jnp.int32(8))
    for n in range(3):
        gw9[n] = ninth[128 * n : 128 * n + 128]
        gwb9[n] = ninth[128 * n : 128 * n + 128].astype(BF16)
    first = core == 0
    a9_copy = Copy(
        gwb9, abuf9, a9_s, a9_r, {"space": sibling}, core == 1, first
    ).start()

    gi_copies = []

    def backward(h):
        acc = jnp.dot(wg[...], patches(gb, h), preferred_element_type=F32)
        total = shift_lanes(acc[0:128], -1) + acc[128:256] + shift_lanes(acc[256:384], 1)
        gout[h] = total.astype(BF16)

    def send_rows(first, count):
        for k in range(1, 8):
            to = pl.ds(pl.multiple_of(16 * chan_peer(k), 16), 16)
            gi_copies.append(Copy(
                gout.at[pl.ds(first, count), to, :], back.at[pl.ds(4 * r + first, count)],
                gi_s, gi_r, {"chan": chan_peer(k)},
            ).start())
        back[pl.ds(4 * r + first, count)] = gout[first : first + count, mine, :]

    drain(gb.at[1:5, :, 640:768], gh_r.at[6], has_hi)
    drain(gb.at[1:5, :, 0:128], gh_r.at[7], has_lo)
    backward(1)
    backward(2)
    send_rows(1, 2)
    a9_copy.wait_recv()

    @pl.when(first)
    def _():
        gw9[...] = gw9[...] + abuf9[...].astype(F32)
        sb9[...] = gw9[...].astype(BF16)

    b9_copies = []
    for k in range(1, 4):
        q = lax.rem(px + k, 4)
        b9_copies.append(Copy(
            sb9.at[lax.min(q, 2)], xbuf9.at[k - 1], b9_s.at[k - 1], b9_r.at[k - 1],
            {"space": x_peer(k)}, jnp.logical_and(first, q < 3), jnp.logical_and(first, px < 3),
        ).start())
    for sent in row_rims:
        for copy in sent:
            copy.wait_recv()
    backward(0)
    backward(3)

    total = pair_sum(3)
    drain(xbuf, b_r)
    for j in range(3):
        total = total + xbuf[j].astype(F32)
    for slot in range(3):
        yb[slot] = total[slot].T.astype(BF16)
    yb[3] = jnp.zeros((128, 128), BF16)
    for copy in b9_copies:
        copy.wait_recv()

    @pl.when(jnp.logical_and(first, px < 3))
    def _():
        total9 = gw9[lax.min(px, 2)]
        for j in range(3):
            total9 = total9 + xbuf9[j].astype(F32)
        yb[3] = total9.T.astype(BF16)

    y_copies = []
    for dz in range(2):
        for k in range(8):
            if dz or k:
                z, to = lax.rem(pz + dz, 2), chan_peer(k)
                y_copies.append(Copy(
                    yb.at[:, pl.ds(pl.multiple_of(16 * to, 16), 16), :], ybuf.at[8 * pz + c],
                    y_s, y_r, {"space": 8 * z + 2 * px + core, "chan": to},
                ).start())
    ybuf[8 * pz + c] = yb[:, mine, :]
    send_rows(0, 1)
    send_rows(3, 1)
    drain(ybuf.at[0:15], y_r)
    total = ybuf[0].astype(F32)
    for n in range(1, 16):
        total = total + ybuf[n].astype(F32)
    piece = gwf.at[4 * core + px]
    piece[...] = total.astype(BF16)
    d_copies = [
        Copy(piece, piece, d_s, d_r, {"space": half_peer(k)}).start()
        for k in range(1, 8)
    ]
    drain(back.at[0:28], gi_r)
    for d in range(4):
        for h in range(32):
            wide[24 * h : 24 * h + 16, :] = back[h, :, 128 * d : 128 * d + 128].astype(F32)

        def step(ch, _):
            gi_ref[ch, d] = wide[pl.ds(ch, 32, stride=24), :].astype(BF16)
            return 0

        lax.fori_loop(0, 16, step, 0)
    out = pltpu.make_async_copy(gi_ref, gi_hbm, io_sem.at[0])
    out.start()
    drain(fp.at[0:28], wy_s, some)
    drain(xb.at[:, 0:112, 128:640], x_s)
    drain(ct.at[:, 0:112, :], t_s)
    drain(wall.at[0:12], wx_s, some)
    drain(wall.at[0:16], wd_s, core == 0)
    drain(wall.at[0:12], wd_s, core == 1)
    drain(xb.at[:, :, 128:256], xh_s.at[0], has_lo)
    drain(xb.at[:, :, 512:640], xh_s.at[1], has_hi)
    drain(gb.at[1:5, :, 128:256], gh_s.at[6], has_lo)
    drain(gb.at[1:5, :, 512:640], gh_s.at[7], has_hi)
    drain(back.at[0:28], gi_s)
    drain(gwb.at[0:4], a_s)
    drain(sb, b_s)
    drain(ybuf.at[0:15], y_s)
    for copy in row_rims[0] + row_rims[1] + [a9_copy] + b9_copies:
        copy.wait_send()
    drain(gwf.at[0:7], d_r)
    for tap in range(27):
        n, slot = (tap // 3, tap % 3) if tap < 24 else (tap - 24, 3)
        gw_ref[tap] = gwf[n, slot].astype(F32) * scale
    out_w = pltpu.make_async_copy(gw_ref, gw_hbm, io_sem.at[1])
    out_w.start()

    drain(gwf.at[0:7], d_s)
    out.wait()
    out_w.wait()


def body(inputs, filters, cotangent):
    cells = inputs.shape[1] * lax.axis_size("space") * inputs.shape[2] * inputs.shape[3]
    scale = 1.0 / math.sqrt(cells)
    sems = [0, 7, 0, 0, 0, 0, 0, 3, 0, 0, 2, 2, 8, 8, 0, 0, 0, 4, 0, 0, 0, 0, 3, 3, 0, 0, 0, 0, 3]
    scratch = [
        (inputs.shape, BF16),
        (filters.shape, BF16),
        (inputs.shape, BF16),
        (inputs.shape, BF16),
        (filters.shape, F32),
        ((PITCH * 16, 128), F32),
        ((34, 16, 512), BF16),
        ((32, 16, 512), BF16),
        ((32, 16, 128), BF16),
        ((6, 128, 768), BF16),
        ((4, 128, 512), BF16),
        ((32, 128, 128), BF16),
        ((384, 1152), BF16),
        ((384, 1152), BF16),
        ((4, 128, 512), F32),
        ((6, 128, 768), BF16),
        ((4, 384, 512), BF16),
        ((8, 3, 128, 128), F32),
        ((8, 3, 128, 128), BF16),
        ((4, 3, 128, 128), BF16),
        ((3, 3, 128, 128), BF16),
        ((3, 3, 128, 128), BF16),
        ((3, 128, 128), F32),
        ((3, 128, 128), BF16),
        ((3, 128, 128), BF16),
        ((3, 128, 128), BF16),
        ((3, 128, 128), BF16),
        ((4, 128, 128), BF16),
        ((16, 4, 16, 128), BF16),
        ((8, 4, 16, 128), BF16),
        ((4, 128, 512), BF16),
        ((32, 16, 512), BF16),
    ]
    hbm = pl.BlockSpec(memory_space=pl.ANY)
    return pl.pallas_call(
        lambda *refs: kernel(scale, *refs),
        out_shape=(
            jax.ShapeDtypeStruct(inputs.shape, BF16),
            jax.ShapeDtypeStruct(filters.shape, F32),
        ),
        in_specs=[hbm] * 3,
        out_specs=(hbm, hbm),
        scratch_shapes=[pltpu.VMEM(s, t) for s, t in scratch]
        + [pltpu.SemaphoreType.DMA((n,) if n else ()) for n in sems],
        compiler_params=pltpu.CompilerParams(
            collective_id=0, has_side_effects=True, vmem_limit_bytes=60 * 2**20
        ),
        name="conv_backward",
    )(inputs, filters, cotangent)


def solution(mesh):
    placed = (P("chan", "space", None, None), P(None, "chan", None), P("chan", "space", None, None))
    return jax.shard_map(
        body,
        mesh=mesh,
        in_specs=placed,
        out_specs=(P("chan", "space", None, None), P(None, "chan", None)),
        check_vma=False,
    )
```

```python
import math

import jax
import jax.numpy as jnp
from jax import lax
from jax.experimental import pallas as pl
from jax.experimental.pallas import tpu as pltpu
from jax.sharding import PartitionSpec as P

MESH = pl.DeviceIdType.MESH
BF16 = jnp.bfloat16
F32 = jnp.float32
PITCH = 136
STEPS = (2, 1, 3, 0)


def row_block(c):
    y = lax.div(c, 2)
    z = lax.rem(c, 2)
    q = lax.rem(y, 2)
    return 2 * y + z + q - 2 * z * q


class Copy:
    def __init__(self, src, dst, send_sem, recv_sem, where, sends=None, gets=None):
        self.copy = pltpu.make_async_remote_copy(
            src_ref=src, dst_ref=dst, send_sem=send_sem, recv_sem=recv_sem,
            device_id=where, device_id_type=MESH,
        )
        self.sends, self.gets = sends, gets

    def start(self):
        self.copy.start() if self.sends is None else pl.when(self.sends)(self.copy.start)
        return self

    def wait_recv(self):
        self.copy.wait_recv() if self.gets is None else pl.when(self.gets)(self.copy.wait_recv)

    def wait_send(self):
        self.copy.wait_send() if self.sends is None else pl.when(self.sends)(self.copy.wait_send)


def drain(like, sem, when=None):
    wait = pltpu.make_async_copy(like, like, sem).wait
    wait() if when is None else pl.when(when)(wait)


def shift_lanes(block, by):
    lane = lax.broadcasted_iota(jnp.int32, (block.shape[0], 128), 1)
    edge = 0 if by == 1 else 127
    pieces = []
    for d in range(block.shape[1] // 128):
        rolled = pltpu.roll(block[:, 128 * d : 128 * d + 128], by % 128, 1)
        pieces.append(jnp.where(lane == edge, 0.0, rolled))
    return jnp.concatenate(pieces, axis=1)


def kernel(
    scale, x_hbm, f_hbm, t_hbm, gi_hbm, gw_hbm,
    x_ref, f_ref, t_ref, gi_ref, gw_ref, wide, xt, tt, fp, xb, ct, wall, wg, wf, pre, xtt, gb, gs, gw, gwb, abuf, sb, xbuf,
    gw9, gwb9, abuf9, sb9, xbuf9, yb, ybuf, gwf,
    gout, back,
    x_s, x_r, t_s, t_r, wy_s, wy_r, wx_s, wx_r, wd_s, wd_r, xh_s, xh_r, gh_s, gh_r, gi_s, gi_r,
    a_s, a_r, a9_s, a9_r, b_s, b_r, b9_s, b9_r, y_s, y_r, d_s, d_r, io_sem,
):
    c = lax.axis_index("chan")
    g = lax.axis_index("space")
    r = row_block(c)
    core = lax.rem(g, 2)
    px = lax.rem(lax.div(g, 2), 4)
    pz = lax.div(g, 8)
    sibling = g + 1 - 2 * core
    mine = pl.ds(pl.multiple_of(16 * c, 16), 16)
    has_lo, has_hi = g > 0, g < 15
    has_up, has_down = r > 0, r < 7

    def chan_peer(k):
        return lax.rem(c + k, 8)

    def x_peer(k):
        return 8 * pz + 2 * lax.rem(px + k, 4) + core

    def half_peer(k):
        return 8 * pz + lax.rem(2 * px + core + k, 8)

    barrier = pltpu.get_barrier_semaphore()
    for k in range(1, 8):
        pl.semaphore_signal(barrier, inc=1, device_id={"chan": chan_peer(k)}, device_id_type=MESH)
    for k in range(1, 8):
        pl.semaphore_signal(barrier, inc=1, device_id={"space": half_peer(k)}, device_id_type=MESH)
    for k in range(8):
        pl.semaphore_signal(
            barrier, inc=1, device_id={"space": lax.rem(g + 8, 16), "chan": chan_peer(k)},
            device_id_type=MESH,
        )
    for edge, dg in ((7, 1), (8, -1)):

        @pl.when(g == edge)
        def _():
            pl.semaphore_signal(barrier, inc=1, device_id={"space": g + dg}, device_id_type=MESH)

    for dg, has_g in ((-1, has_lo), (1, has_hi)):
        for dr, has_r in ((-1, has_up), (1, has_down)):

            @pl.when(jnp.logical_and(has_g, has_r))
            def _():
                pl.semaphore_signal(
                    barrier, inc=1,
                    device_id={"space": g + dg, "chan": row_block(r + dr)}, device_id_type=MESH,
                )

    loads = [
        pltpu.make_async_copy(src, dst, io_sem.at[n])
        for n, (src, dst) in enumerate(((x_hbm, x_ref), (f_hbm, f_ref), (t_hbm, t_ref)))
    ]
    for load in loads:
        load.start()

    xt[0] = jnp.zeros((16, 512), BF16)
    xt[33] = jnp.zeros((16, 512), BF16)

    @pl.when(g == 0)
    def _():
        xb[:, :, 0:128] = jnp.zeros((6, 128, 128), BF16)
        gb[:, :, 0:128] = jnp.zeros((6, 128, 128), BF16)

    @pl.when(g == 15)
    def _():
        xb[:, :, 640:768] = jnp.zeros((6, 128, 128), BF16)
        gb[:, :, 640:768] = jnp.zeros((6, 128, 128), BF16)

    @pl.when(r == 0)
    def _():
        gb[0] = jnp.zeros((128, 768), BF16)

    @pl.when(r == 7)
    def _():
        gb[5] = jnp.zeros((128, 768), BF16)


    def to_rows(src, dst, first):
        for ch in range(16):
            wide[PITCH * ch : PITCH * ch + 128, :] = src[ch].reshape(128, 128).astype(F32)

        def step(h, _):
            for d in range(4):
                rows = wide[pl.ds(32 * d + h, 16, stride=PITCH), :]
                dst[first + h, :, 128 * d : 128 * d + 128] = rows.astype(BF16)
            return 0

        lax.fori_loop(0, 32, step, 0)

    loads[0].wait()
    to_rows(x_ref, xt, 1)
    sides_g = has_lo.astype(jnp.int32) + has_hi.astype(jnp.int32)
    sides_r = has_up.astype(jnp.int32) + has_down.astype(jnp.int32)
    middle = (g == 7).astype(jnp.int32) + (g == 8).astype(jnp.int32)
    loads[1].wait()
    fp[0:27] = f_ref[...]
    fp[27:32] = jnp.zeros((5, 16, 128), BF16)
    pl.semaphore_wait(barrier, 22 + middle + sides_g * sides_r)

    part = 4 * (4 * core + px)
    some = part < 28
    wy_copies = [
        Copy(
            fp.at[pl.ds(part, 4)], wall.at[pl.ds(part, 4), mine, :],
            wy_s, wy_r, {"chan": chan_peer(k)}, some, some,
        ).start()
        for k in range(1, 8)
    ]
    wall[pl.ds(part, 4), mine, :] = fp[pl.ds(part, 4)]
    x_copies = [
        Copy(
            xt.at[pl.ds(4 * row_block(chan_peer(k)), 6)], xb.at[:, mine, 128:640],
            x_s, x_r.at[k - 1], {"chan": chan_peer(k)},
        ).start()
        for k in range(1, 8)
    ]
    xb[:, mine, 128:640] = xt[pl.ds(4 * r, 6)]
    loads[2].wait()
    to_rows(t_ref, tt, 0)
    t_copies = [
        Copy(
            tt.at[pl.ds(4 * row_block(chan_peer(k)), 4)], ct.at[:, mine, :],
            t_s, t_r, {"chan": chan_peer(k)},
        ).start()
        for k in range(1, 8)
    ]
    ct[:, mine, :] = tt[pl.ds(4 * r, 4)]
    drain(fp.at[0:28], wy_r, some)
    wx_copies = [
        Copy(
            wall.at[pl.ds(part, 4)], wall.at[pl.ds(part, 4)],
            wx_s, wx_r.at[k - 1], {"space": x_peer(k)},
            some, core + lax.rem(px + 4 - k, 4) < 4,
        ).start()
        for k in range(1, 4)
    ]

    wd_copies = []

    def pass_filters(k):
        owner = lax.rem(px + 4 - k, 4)
        piece = wall.at[pl.ds(4 * (4 * core + owner), 4)]
        wd_copies.append(Copy(
            piece, piece, wd_s, wd_r, {"space": sibling},
            core + owner < 4, 1 - core + owner < 4,
        ).start())

    pass_filters(0)

    h_copies = []

    def pass_rims(k):
        rows = pl.ds(pl.multiple_of(16 * lax.rem(c + 8 - k, 8), 16), 16)
        for n, at, to, dg in ((0, 128, 640, -1), (1, 512, 0, 1)):
            has_g, from_g = (has_lo, has_hi) if dg < 0 else (has_hi, has_lo)
            h_copies.append(Copy(
                xb.at[:, rows, at : at + 128], xb.at[:, rows, to : to + 128],
                xh_s.at[n], xh_r.at[n], {"space": g + dg}, has_g, from_g,
            ).start())

    pass_rims(0)
    for k in range(1, 6):
        x_copies[k - 1].wait_recv()
        pass_rims(k)
    for k in range(1, 4):
        wx_copies[k - 1].wait_recv()
        pass_filters(k)
    for k in range(6, 8):
        x_copies[k - 1].wait_recv()
        pass_rims(k)
    drain(wall.at[0:12], wd_r, core == 0)
    drain(wall.at[0:16], wd_r, core == 1)
    for tap in range(27):
        a, b, cc = tap // 9, tap // 3 % 3, tap % 3
        block = wall[tap]
        rows = slice(128 * cc, 128 * cc + 128)
        wg[rows, 128 * (8 - 3 * a - b) : 128 * (9 - 3 * a - b)] = block
        wf[rows, 128 * (3 * a + b) : 128 * (3 * a + b + 1)] = block.T
    drain(xb.at[:, :, 640:768], xh_r.at[0], has_hi)
    drain(xb.at[:, :, 0:128], xh_r.at[1], has_lo)

    def patches(src, h):
        rows = [src[h + b, :, 128 * a : 128 * a + 512] for a in range(3) for b in range(3)]
        return jnp.concatenate(rows, axis=0)

    def forward(h, _):
        acc = jnp.dot(wf[...], patches(xb, h), preferred_element_type=F32)
        pre[h] = shift_lanes(acc[0:128], 1) + acc[128:256] + shift_lanes(acc[256:384], -1)
        for n in range(9):
            row, plane = lax.div(9 * h + n, 6), lax.rem(9 * h + n, 6)
            at = pl.ds(pl.multiple_of(128 * plane, 128), 128)
            xtt[row, at, :] = xb[row, :, at].T
        return 0

    lax.fori_loop(0, 4, forward, 0)
    drain(ct.at[:, 0:112, :], t_r)

    up, down = row_block(lax.max(r - 1, 0)), row_block(lax.min(r + 1, 7))
    row_rims, plane_rims = [], []

    def send_rims(row, to_row, has_r, from_r, to):
        n = 3 * len(row_rims)
        sent = [Copy(
            gb.at[row, :, 128:640], gb.at[to_row, :, 128:640], gh_s.at[n], gh_r.at[n],
            {"chan": to}, has_r, from_r,
        ).start()]
        for m, plane, to_plane, dg in ((1, 128, 640, -1), (2, 512, 0, 1)):
            has_g, from_g = (has_lo, has_hi) if dg < 0 else (has_hi, has_lo)
            sent.append(Copy(
                gb.at[row, :, plane : plane + 128], gb.at[to_row, :, to_plane : to_plane + 128],
                gh_s.at[n + m], gh_r.at[n + m], {"space": g + dg, "chan": to},
                jnp.logical_and(has_g, has_r), jnp.logical_and(from_g, from_r),
            ).start())
        row_rims.append(sent)

    for h in (0, 3, 1, 2):
        p = pre[h]
        sigma = 1.0 / (1.0 + jnp.exp(-p))
        grad = ct[h].astype(F32) * sigma * (1.0 + p * (1.0 - sigma))
        gb[h + 1, :, 128:640] = grad.astype(BF16)
        for n, at, to, dg in ((6, 128, 640, -1), (7, 512, 0, 1)):
            has_g, from_g = (has_lo, has_hi) if dg < 0 else (has_hi, has_lo)
            plane_rims.append(Copy(
                gb.at[h + 1, :, at : at + 128], gb.at[h + 1, :, to : to + 128],
                gh_s.at[n], gh_r.at[n], {"space": g + dg}, has_g, from_g,
            ).start())
        if h == 0:
            send_rims(1, 5, has_up, has_down, up)
        if h == 3:
            send_rims(4, 0, has_down, has_up, down)
        gs[h, 0:128, :] = shift_lanes(grad, -1).astype(BF16)
        gs[h, 128:256, :] = grad.astype(BF16)
        gs[h, 256:384, :] = shift_lanes(grad, 1).astype(BF16)

    grads = jnp.concatenate([gs[h] for h in range(4)], axis=1)

    def product(*offsets):
        sides = []
        for ab in offsets:
            lanes = pl.ds(pl.multiple_of(128 * lax.div(ab, 3), 128), 512)
            rows = [xtt[h + lax.rem(ab, 3), lanes, :] for h in range(4)]
            sides.append(jnp.concatenate(rows, axis=0))
        side = sides[0] if len(sides) == 1 else jnp.concatenate(sides, axis=1)
        return jnp.dot(grads, side, preferred_element_type=F32)

    a_copies, b_copies = [], []
    first = core == 0

    def pair_sum(j):
        a_copies[j].wait_recv()
        q = lax.rem(px + STEPS[j], 4)
        total = gw[4 * core + q] + abuf[j].astype(F32)
        if STEPS[j] == 0:
            return total
        sb[j] = total.astype(BF16)
        b_copies.append(Copy(
            sb.at[j], xbuf.at[j], b_s, b_r, {"space": x_peer(STEPS[j])}
        ).start())

    for j in range(4):
        q = lax.rem(px + STEPS[j], 4)
        prod = product(q, q + 4)
        for cc in range(3):
            for n in range(2):
                block = prod[128 * cc : 128 * cc + 128, 128 * n : 128 * n + 128]
                gw[4 * n + q, cc] = block
                gwb[4 * n + q, cc] = block.astype(BF16)
        a_copies.append(Copy(
            gwb.at[4 * (1 - core) + q], abuf.at[j], a_s, a_r.at[j], {"space": sibling}
        ).start())
        if j == 1:
            ninth = product(jnp.int32(8))
            for n in range(3):
                gw9[n] = ninth[128 * n : 128 * n + 128]
                gwb9[n] = ninth[128 * n : 128 * n + 128].astype(BF16)
            a9_copy = Copy(
                gwb9, abuf9, a9_s, a9_r, {"space": sibling}, core == 1, first
            ).start()
        if j:
            pair_sum(j - 1)
    a9_copy.wait_recv()

    @pl.when(first)
    def _():
        gw9[...] = gw9[...] + abuf9[...].astype(F32)
        sb9[...] = gw9[...].astype(BF16)

    b9_copies = []
    for k in range(1, 4):
        q = lax.rem(px + k, 4)
        b9_copies.append(Copy(
            sb9.at[lax.min(q, 2)], xbuf9.at[k - 1], b9_s.at[k - 1], b9_r.at[k - 1],
            {"space": x_peer(k)}, jnp.logical_and(first, q < 3), jnp.logical_and(first, px < 3),
        ).start())

    gi_copies = []

    def backward(h):
        acc = jnp.dot(wg[...], patches(gb, h), preferred_element_type=F32)
        total = shift_lanes(acc[0:128], -1) + acc[128:256] + shift_lanes(acc[256:384], 1)
        gout[h] = total.astype(BF16)

    def send_rows(first, count):
        for k in range(1, 8):
            to = pl.ds(pl.multiple_of(16 * chan_peer(k), 16), 16)
            gi_copies.append(Copy(
                gout.at[pl.ds(first, count), to, :], back.at[pl.ds(4 * r + first, count)],
                gi_s, gi_r, {"chan": chan_peer(k)},
            ).start())
        back[pl.ds(4 * r + first, count)] = gout[first : first + count, mine, :]

    drain(gb.at[1:5, :, 640:768], gh_r.at[6], has_hi)
    drain(gb.at[1:5, :, 0:128], gh_r.at[7], has_lo)
    backward(1)
    backward(2)
    send_rows(1, 2)
    for sent in row_rims:
        for copy in sent:
            copy.wait_recv()
    backward(0)
    backward(3)

    total = pair_sum(3)
    drain(xbuf, b_r)
    for j in range(3):
        total = total + xbuf[j].astype(F32)
    for slot in range(3):
        yb[slot] = total[slot].T.astype(BF16)
    yb[3] = jnp.zeros((128, 128), BF16)
    for copy in b9_copies:
        copy.wait_recv()

    @pl.when(jnp.logical_and(first, px < 3))
    def _():
        total9 = gw9[lax.min(px, 2)]
        for j in range(3):
            total9 = total9 + xbuf9[j].astype(F32)
        yb[3] = total9.T.astype(BF16)

    y_copies = []
    for dz in range(2):
        for k in range(8):
            if dz or k:
                z, to = lax.rem(pz + dz, 2), chan_peer(k)
                y_copies.append(Copy(
                    yb.at[:, pl.ds(pl.multiple_of(16 * to, 16), 16), :], ybuf.at[8 * pz + c],
                    y_s, y_r, {"space": 8 * z + 2 * px + core, "chan": to},
                ).start())
    ybuf[8 * pz + c] = yb[:, mine, :]
    send_rows(0, 1)
    send_rows(3, 1)
    drain(ybuf.at[0:15], y_r)
    total = ybuf[0].astype(F32)
    for n in range(1, 16):
        total = total + ybuf[n].astype(F32)
    piece = gwf.at[4 * core + px]
    piece[...] = total.astype(BF16)
    d_copies = [
        Copy(piece, piece, d_s, d_r, {"space": half_peer(k)}).start()
        for k in range(1, 8)
    ]
    drain(back.at[0:28], gi_r)
    for d in range(4):
        for h in range(32):
            wide[24 * h : 24 * h + 16, :] = back[h, :, 128 * d : 128 * d + 128].astype(F32)

        def step(ch, _):
            gi_ref[ch, d] = wide[pl.ds(ch, 32, stride=24), :].astype(BF16)
            return 0

        lax.fori_loop(0, 16, step, 0)
    out = pltpu.make_async_copy(gi_ref, gi_hbm, io_sem.at[0])
    out.start()
    drain(fp.at[0:28], wy_s, some)
    drain(xb.at[:, 0:112, 128:640], x_s)
    drain(ct.at[:, 0:112, :], t_s)
    drain(wall.at[0:12], wx_s, some)
    drain(wall.at[0:16], wd_s, core == 0)
    drain(wall.at[0:12], wd_s, core == 1)
    drain(xb.at[:, :, 128:256], xh_s.at[0], has_lo)
    drain(xb.at[:, :, 512:640], xh_s.at[1], has_hi)
    drain(gb.at[1:5, :, 128:256], gh_s.at[6], has_lo)
    drain(gb.at[1:5, :, 512:640], gh_s.at[7], has_hi)
    drain(back.at[0:28], gi_s)
    drain(gwb.at[0:4], a_s)
    drain(sb, b_s)
    drain(ybuf.at[0:15], y_s)
    for copy in row_rims[0] + row_rims[1] + [a9_copy] + b9_copies:
        copy.wait_send()
    drain(gwf.at[0:7], d_r)
    for tap in range(27):
        n, slot = (tap // 3, tap % 3) if tap < 24 else (tap - 24, 3)
        gw_ref[tap] = gwf[n, slot].astype(F32) * scale
    out_w = pltpu.make_async_copy(gw_ref, gw_hbm, io_sem.at[1])
    out_w.start()

    drain(gwf.at[0:7], d_s)
    out.wait()
    out_w.wait()


def body(inputs, filters, cotangent):
    cells = inputs.shape[1] * lax.axis_size("space") * inputs.shape[2] * inputs.shape[3]
    scale = 1.0 / math.sqrt(cells)
    sems = [0, 7, 0, 0, 0, 0, 0, 3, 0, 0, 2, 2, 8, 8, 0, 0, 0, 4, 0, 0, 0, 0, 3, 3, 0, 0, 0, 0, 3]
    scratch = [
        (inputs.shape, BF16),
        (filters.shape, BF16),
        (inputs.shape, BF16),
        (inputs.shape, BF16),
        (filters.shape, F32),
        ((PITCH * 16, 128), F32),
        ((34, 16, 512), BF16),
        ((32, 16, 512), BF16),
        ((32, 16, 128), BF16),
        ((6, 128, 768), BF16),
        ((4, 128, 512), BF16),
        ((32, 128, 128), BF16),
        ((384, 1152), BF16),
        ((384, 1152), BF16),
        ((4, 128, 512), F32),
        ((6, 768, 128), BF16),
        ((6, 128, 768), BF16),
        ((4, 384, 512), BF16),
        ((8, 3, 128, 128), F32),
        ((8, 3, 128, 128), BF16),
        ((4, 3, 128, 128), BF16),
        ((3, 3, 128, 128), BF16),
        ((3, 3, 128, 128), BF16),
        ((3, 128, 128), F32),
        ((3, 128, 128), BF16),
        ((3, 128, 128), BF16),
        ((3, 128, 128), BF16),
        ((3, 128, 128), BF16),
        ((4, 128, 128), BF16),
        ((16, 4, 16, 128), BF16),
        ((8, 4, 16, 128), BF16),
        ((4, 128, 512), BF16),
        ((32, 16, 512), BF16),
    ]
    hbm = pl.BlockSpec(memory_space=pl.ANY)
    return pl.pallas_call(
        lambda *refs: kernel(scale, *refs),
        out_shape=(
            jax.ShapeDtypeStruct(inputs.shape, BF16),
            jax.ShapeDtypeStruct(filters.shape, F32),
        ),
        in_specs=[hbm] * 3,
        out_specs=(hbm, hbm),
        scratch_shapes=[pltpu.VMEM(s, t) for s, t in scratch]
        + [pltpu.SemaphoreType.DMA((n,) if n else ()) for n in sems],
        compiler_params=pltpu.CompilerParams(
            collective_id=0, has_side_effects=True, vmem_limit_bytes=60 * 2**20
        ),
        name="conv_backward",
    )(inputs, filters, cotangent)


def solution(mesh):
    placed = (P("chan", "space", None, None), P(None, "chan", None), P("chan", "space", None, None))
    return jax.shard_map(
        body,
        mesh=mesh,
        in_specs=placed,
        out_specs=(P("chan", "space", None, None), P(None, "chan", None)),
        check_vma=False,
    )
```

```python
import math

import jax
import jax.numpy as jnp
from jax import lax
from jax.experimental import pallas as pl
from jax.experimental.pallas import tpu as pltpu
from jax.sharding import PartitionSpec as P

MESH = pl.DeviceIdType.MESH
BF16 = jnp.bfloat16
F32 = jnp.float32
PITCH = 136
STEPS = (2, 1, 3, 0)


def row_block(c):
    y = lax.div(c, 2)
    z = lax.rem(c, 2)
    q = lax.rem(y, 2)
    return 2 * y + z + q - 2 * z * q


class Copy:
    def __init__(self, src, dst, send_sem, recv_sem, where, sends=None, gets=None):
        self.copy = pltpu.make_async_remote_copy(
            src_ref=src, dst_ref=dst, send_sem=send_sem, recv_sem=recv_sem,
            device_id=where, device_id_type=MESH,
        )
        self.sends, self.gets = sends, gets

    def start(self):
        self.copy.start() if self.sends is None else pl.when(self.sends)(self.copy.start)
        return self

    def wait_recv(self):
        self.copy.wait_recv() if self.gets is None else pl.when(self.gets)(self.copy.wait_recv)

    def wait_send(self):
        self.copy.wait_send() if self.sends is None else pl.when(self.sends)(self.copy.wait_send)


def drain(like, sem, when=None):
    wait = pltpu.make_async_copy(like, like, sem).wait
    wait() if when is None else pl.when(when)(wait)


def shift_lanes(block, by):
    lane = lax.broadcasted_iota(jnp.int32, (block.shape[0], 128), 1)
    edge = 0 if by == 1 else 127
    pieces = []
    for d in range(block.shape[1] // 128):
        rolled = pltpu.roll(block[:, 128 * d : 128 * d + 128], by % 128, 1)
        pieces.append(jnp.where(lane == edge, 0.0, rolled))
    return jnp.concatenate(pieces, axis=1)


def kernel(
    scale, x_hbm, f_hbm, t_hbm, gi_hbm, gw_hbm,
    x_ref, f_ref, t_ref, gi_ref, gw_ref, wide, xt, tt, fp, xb, ct, wall, wg, wf, pre, xtt, gb, gs, gw, gwb, abuf, sb, xbuf,
    gw9, gwb9, abuf9, sb9, xbuf9, yb, ybuf, gwf,
    gout, back,
    x_s, x_r, t_s, t_r, wy_s, wy_r, wx_s, wx_r, wd_s, wd_r, xh_s, xh_r, gh_s, gh_r, gi_s, gi_r,
    a_s, a_r, a9_s, a9_r, b_s, b_r, b9_s, b9_r, y_s, y_r, d_s, d_r, io_sem,
):
    c = lax.axis_index("chan")
    g = lax.axis_index("space")
    r = row_block(c)
    core = lax.rem(g, 2)
    px = lax.rem(lax.div(g, 2), 4)
    pz = lax.div(g, 8)
    sibling = g + 1 - 2 * core
    mine = pl.ds(pl.multiple_of(16 * c, 16), 16)
    has_lo, has_hi = g > 0, g < 15
    has_up, has_down = r > 0, r < 7

    def chan_peer(k):
        return lax.rem(c + k, 8)

    def x_peer(k):
        return 8 * pz + 2 * lax.rem(px + k, 4) + core

    def half_peer(k):
        return 8 * pz + lax.rem(2 * px + core + k, 8)

    barrier = pltpu.get_barrier_semaphore()
    for k in range(1, 8):
        pl.semaphore_signal(barrier, inc=1, device_id={"chan": chan_peer(k)}, device_id_type=MESH)
    for k in range(1, 8):
        pl.semaphore_signal(barrier, inc=1, device_id={"space": half_peer(k)}, device_id_type=MESH)
    for k in range(8):
        pl.semaphore_signal(
            barrier, inc=1, device_id={"space": lax.rem(g + 8, 16), "chan": chan_peer(k)},
            device_id_type=MESH,
        )
    for edge, dg in ((7, 1), (8, -1)):

        @pl.when(g == edge)
        def _():
            pl.semaphore_signal(barrier, inc=1, device_id={"space": g + dg}, device_id_type=MESH)

    for dg, has_g in ((-1, has_lo), (1, has_hi)):
        for dr, has_r in ((-1, has_up), (1, has_down)):

            @pl.when(jnp.logical_and(has_g, has_r))
            def _():
                pl.semaphore_signal(
                    barrier, inc=1,
                    device_id={"space": g + dg, "chan": row_block(r + dr)}, device_id_type=MESH,
                )

    loads = [
        pltpu.make_async_copy(src, dst, io_sem.at[n])
        for n, (src, dst) in enumerate(((x_hbm, x_ref), (f_hbm, f_ref), (t_hbm, t_ref)))
    ]
    for load in loads:
        load.start()

    xt[0] = jnp.zeros((16, 512), BF16)
    xt[33] = jnp.zeros((16, 512), BF16)

    @pl.when(g == 0)
    def _():
        xb[:, :, 0:128] = jnp.zeros((6, 128, 128), BF16)
        gb[:, :, 0:128] = jnp.zeros((6, 128, 128), BF16)

    @pl.when(g == 15)
    def _():
        xb[:, :, 640:768] = jnp.zeros((6, 128, 128), BF16)
        gb[:, :, 640:768] = jnp.zeros((6, 128, 128), BF16)

    @pl.when(r == 0)
    def _():
        gb[0] = jnp.zeros((128, 768), BF16)

    @pl.when(r == 7)
    def _():
        gb[5] = jnp.zeros((128, 768), BF16)


    def to_rows(src, dst, first):
        for ch in range(16):
            wide[PITCH * ch : PITCH * ch + 128, :] = src[ch].reshape(128, 128).astype(F32)

        def step(h, _):
            for d in range(4):
                rows = wide[pl.ds(32 * d + h, 16, stride=PITCH), :]
                dst[first + h, :, 128 * d : 128 * d + 128] = rows.astype(BF16)
            return 0

        lax.fori_loop(0, 32, step, 0)

    loads[0].wait()
    to_rows(x_ref, xt, 1)
    sides_g = has_lo.astype(jnp.int32) + has_hi.astype(jnp.int32)
    sides_r = has_up.astype(jnp.int32) + has_down.astype(jnp.int32)
    middle = (g == 7).astype(jnp.int32) + (g == 8).astype(jnp.int32)
    loads[1].wait()
    fp[0:27] = f_ref[...]
    fp[27:32] = jnp.zeros((5, 16, 128), BF16)
    pl.semaphore_wait(barrier, 22 + middle + sides_g * sides_r)

    part = 4 * (4 * core + px)
    some = part < 28
    wy_copies = [
        Copy(
            fp.at[pl.ds(part, 4)], wall.at[pl.ds(part, 4), mine, :],
            wy_s, wy_r, {"chan": chan_peer(k)}, some, some,
        ).start()
        for k in range(1, 8)
    ]
    wall[pl.ds(part, 4), mine, :] = fp[pl.ds(part, 4)]
    x_copies = [
        Copy(
            xt.at[pl.ds(4 * row_block(chan_peer(k)), 6)], xb.at[:, mine, 128:640],
            x_s, x_r.at[k - 1], {"chan": chan_peer(k)},
        ).start()
        for k in range(1, 8)
    ]
    xb[:, mine, 128:640] = xt[pl.ds(4 * r, 6)]
    loads[2].wait()
    to_rows(t_ref, tt, 0)
    t_copies = [
        Copy(
            tt.at[pl.ds(4 * row_block(chan_peer(k)), 4)], ct.at[:, mine, :],
            t_s, t_r, {"chan": chan_peer(k)},
        ).start()
        for k in range(1, 8)
    ]
    ct[:, mine, :] = tt[pl.ds(4 * r, 4)]
    drain(fp.at[0:28], wy_r, some)
    wx_copies = [
        Copy(
            wall.at[pl.ds(part, 4)], wall.at[pl.ds(part, 4)],
            wx_s, wx_r.at[k - 1], {"space": x_peer(k)},
            some, core + lax.rem(px + 4 - k, 4) < 4,
        ).start()
        for k in range(1, 4)
    ]

    wd_copies = []

    def pass_filters(k):
        owner = lax.rem(px + 4 - k, 4)
        piece = wall.at[pl.ds(4 * (4 * core + owner), 4)]
        wd_copies.append(Copy(
            piece, piece, wd_s, wd_r, {"space": sibling},
            core + owner < 4, 1 - core + owner < 4,
        ).start())

    pass_filters(0)

    h_copies = []

    def pass_rims(k):
        rows = pl.ds(pl.multiple_of(16 * lax.rem(c + 8 - k, 8), 16), 16)
        for n, at, to, dg in ((0, 128, 640, -1), (1, 512, 0, 1)):
            has_g, from_g = (has_lo, has_hi) if dg < 0 else (has_hi, has_lo)
            h_copies.append(Copy(
                xb.at[:, rows, at : at + 128], xb.at[:, rows, to : to + 128],
                xh_s.at[n], xh_r.at[n], {"space": g + dg}, has_g, from_g,
            ).start())

    pass_rims(0)
    for k in range(1, 6):
        x_copies[k - 1].wait_recv()
        pass_rims(k)
    for k in range(1, 4):
        wx_copies[k - 1].wait_recv()
        pass_filters(k)
    for k in range(6, 8):
        x_copies[k - 1].wait_recv()
        pass_rims(k)
    drain(wall.at[0:12], wd_r, core == 0)
    drain(wall.at[0:16], wd_r, core == 1)
    for tap in range(27):
        a, b, cc = tap // 9, tap // 3 % 3, tap % 3
        block = wall[tap]
        rows = slice(128 * cc, 128 * cc + 128)
        wg[rows, 128 * (8 - 3 * a - b) : 128 * (9 - 3 * a - b)] = block
        wf[rows, 128 * (3 * a + b) : 128 * (3 * a + b + 1)] = block.T
    drain(xb.at[:, :, 640:768], xh_r.at[0], has_hi)
    drain(xb.at[:, :, 0:128], xh_r.at[1], has_lo)

    def patches(src, h):
        rows = [src[h + b, :, 128 * a : 128 * a + 512] for a in range(3) for b in range(3)]
        return jnp.concatenate(rows, axis=0)

    def forward(h, _):
        acc = jnp.dot(wf[...], patches(xb, h), preferred_element_type=F32)
        pre[h] = shift_lanes(acc[0:128], 1) + acc[128:256] + shift_lanes(acc[256:384], -1)
        for n in range(9):
            row, plane = lax.div(9 * h + n, 6), lax.rem(9 * h + n, 6)
            at = pl.ds(pl.multiple_of(128 * plane, 128), 128)
            xtt[row, at, :] = xb[row, :, at].T
        return 0

    lax.fori_loop(0, 4, forward, 0)
    drain(ct.at[:, 0:112, :], t_r)

    up, down = row_block(lax.max(r - 1, 0)), row_block(lax.min(r + 1, 7))
    row_rims, plane_rims = [], []

    def send_rims(row, to_row, has_r, from_r, to):
        n = 3 * len(row_rims)
        sent = [Copy(
            gb.at[row, :, 128:640], gb.at[to_row, :, 128:640], gh_s.at[n], gh_r.at[n],
            {"chan": to}, has_r, from_r,
        ).start()]
        for m, plane, to_plane, dg in ((1, 128, 640, -1), (2, 512, 0, 1)):
            has_g, from_g = (has_lo, has_hi) if dg < 0 else (has_hi, has_lo)
            sent.append(Copy(
                gb.at[row, :, plane : plane + 128], gb.at[to_row, :, to_plane : to_plane + 128],
                gh_s.at[n + m], gh_r.at[n + m], {"space": g + dg, "chan": to},
                jnp.logical_and(has_g, has_r), jnp.logical_and(from_g, from_r),
            ).start())
        row_rims.append(sent)

    for h in (0, 3, 1, 2):
        p = pre[h]
        sigma = 1.0 / (1.0 + jnp.exp(-p))
        grad = ct[h].astype(F32) * sigma * (1.0 + p * (1.0 - sigma))
        gb[h + 1, :, 128:640] = grad.astype(BF16)
        for n, at, to, dg in ((6, 128, 640, -1), (7, 512, 0, 1)):
            has_g, from_g = (has_lo, has_hi) if dg < 0 else (has_hi, has_lo)
            plane_rims.append(Copy(
                gb.at[h + 1, :, at : at + 128], gb.at[h + 1, :, to : to + 128],
                gh_s.at[n], gh_r.at[n], {"space": g + dg}, has_g, from_g,
            ).start())
        if h == 0:
            send_rims(1, 5, has_up, has_down, up)
        if h == 3:
            send_rims(4, 0, has_down, has_up, down)
        gs[h, 0:128, :] = shift_lanes(grad, -1).astype(BF16)
        gs[h, 128:256, :] = grad.astype(BF16)
        gs[h, 256:384, :] = shift_lanes(grad, 1).astype(BF16)

    grads = jnp.concatenate([gs[h] for h in range(4)], axis=1)

    def product(*offsets):
        sides = []
        for ab in offsets:
            lanes = pl.ds(pl.multiple_of(128 * lax.div(ab, 3), 128), 512)
            rows = [xtt[h + lax.rem(ab, 3), lanes, :] for h in range(4)]
            sides.append(jnp.concatenate(rows, axis=0))
        side = sides[0] if len(sides) == 1 else jnp.concatenate(sides, axis=1)
        return jnp.dot(grads, side, preferred_element_type=F32)

    a_copies, b_copies = [], []
    first = core == 0

    def pair_sum(j):
        a_copies[j].wait_recv()
        q = lax.rem(px + STEPS[j], 4)
        total = gw[4 * core + q] + abuf[j].astype(F32)
        if STEPS[j] == 0:
            return total
        sb[j] = total.astype(BF16)
        b_copies.append(Copy(
            sb.at[j], xbuf.at[j], b_s, b_r, {"space": x_peer(STEPS[j])}
        ).start())

    for j in range(4):
        q = lax.rem(px + STEPS[j], 4)
        prod = product(q, q + 4)
        for cc in range(3):
            for n in range(2):
                block = prod[128 * cc : 128 * cc + 128, 128 * n : 128 * n + 128]
                gw[4 * n + q, cc] = block
                gwb[4 * n + q, cc] = block.astype(BF16)
        a_copies.append(Copy(
            gwb.at[4 * (1 - core) + q], abuf.at[j], a_s, a_r.at[j], {"space": sibling}
        ).start())
        if j == 1:
            ninth = product(jnp.int32(8))
            for n in range(3):
                gw9[n] = ninth[128 * n : 128 * n + 128]
                gwb9[n] = ninth[128 * n : 128 * n + 128].astype(BF16)
            a9_copy = Copy(
                gwb9, abuf9, a9_s, a9_r, {"space": sibling}, core == 1, first
            ).start()
        if j:
            pair_sum(j - 1)
    a9_copy.wait_recv()

    @pl.when(first)
    def _():
        gw9[...] = gw9[...] + abuf9[...].astype(F32)
        sb9[...] = gw9[...].astype(BF16)

    b9_copies = []
    for k in range(1, 4):
        q = lax.rem(px + k, 4)
        b9_copies.append(Copy(
            sb9.at[lax.min(q, 2)], xbuf9.at[k - 1], b9_s.at[k - 1], b9_r.at[k - 1],
            {"space": x_peer(k)}, jnp.logical_and(first, q < 3), jnp.logical_and(first, px < 3),
        ).start())

    gi_copies = []

    def backward(h):
        acc = jnp.dot(wg[...], patches(gb, h), preferred_element_type=F32)
        total = shift_lanes(acc[0:128], -1) + acc[128:256] + shift_lanes(acc[256:384], 1)
        gout[h] = total.astype(BF16)

    def send_rows(first, count):
        for k in range(1, 8):
            to = pl.ds(pl.multiple_of(16 * chan_peer(k), 16), 16)
            gi_copies.append(Copy(
                gout.at[pl.ds(first, count), to, :], back.at[pl.ds(4 * r + first, count)],
                gi_s, gi_r, {"chan": chan_peer(k)},
            ).start())
        back[pl.ds(4 * r + first, count)] = gout[first : first + count, mine, :]

    drain(gb.at[1:5, :, 640:768], gh_r.at[6], has_hi)
    drain(gb.at[1:5, :, 0:128], gh_r.at[7], has_lo)
    backward(1)
    backward(2)
    send_rows(1, 2)
    for sent in row_rims:
        for copy in sent:
            copy.wait_recv()
    backward(0)
    backward(3)

    total = pair_sum(3)
    drain(xbuf, b_r)
    for j in range(3):
        total = total + xbuf[j].astype(F32)
    for slot in range(3):
        yb[slot] = total[slot].T.astype(BF16)
    yb[3] = jnp.zeros((128, 128), BF16)
    for copy in b9_copies:
        copy.wait_recv()

    @pl.when(jnp.logical_and(first, px < 3))
    def _():
        total9 = gw9[lax.min(px, 2)]
        for j in range(3):
            total9 = total9 + xbuf9[j].astype(F32)
        yb[3] = total9.T.astype(BF16)

    y_copies = []
    for dz in range(2):
        for k in range(8):
            if dz or k:
                z, to = lax.rem(pz + dz, 2), chan_peer(k)
                y_copies.append(Copy(
                    yb.at[:, pl.ds(pl.multiple_of(16 * to, 16), 16), :], ybuf.at[8 * pz + c],
                    y_s, y_r, {"space": 8 * z + 2 * px + core, "chan": to},
                ).start())
    ybuf[8 * pz + c] = yb[:, mine, :]
    send_rows(0, 1)
    send_rows(3, 1)
    drain(ybuf.at[0:15], y_r)
    total = ybuf[0].astype(F32)
    for n in range(1, 16):
        total = total + ybuf[n].astype(F32)
    piece = gwf.at[4 * core + px]
    piece[...] = total.astype(BF16)
    d_copies = [
        Copy(piece, piece, d_s, d_r, {"space": half_peer(k)}).start()
        for k in range(1, 8)
    ]
    drain(back.at[0:28], gi_r)
    for d in range(4):
        for h in range(32):
            wide[24 * h : 24 * h + 16, :] = back[h, :, 128 * d : 128 * d + 128].astype(F32)

        def step(ch, _):
            gi_ref[ch, d] = wide[pl.ds(ch, 32, stride=24), :].astype(BF16)
            return 0

        lax.fori_loop(0, 16, step, 0)
    out = pltpu.make_async_copy(gi_ref, gi_hbm, io_sem.at[0])
    out.start()
    drain(fp.at[0:28], wy_s, some)
    drain(xb.at[:, 0:112, 128:640], x_s)
    drain(ct.at[:, 0:112, :], t_s)
    drain(wall.at[0:12], wx_s, some)
    drain(wall.at[0:16], wd_s, core == 0)
    drain(wall.at[0:12], wd_s, core == 1)
    drain(xb.at[:, :, 128:256], xh_s.at[0], has_lo)
    drain(xb.at[:, :, 512:640], xh_s.at[1], has_hi)
    drain(gb.at[1:5, :, 128:256], gh_s.at[6], has_lo)
    drain(gb.at[1:5, :, 512:640], gh_s.at[7], has_hi)
    drain(back.at[0:28], gi_s)
    drain(gwb.at[0:4], a_s)
    drain(sb, b_s)
    drain(ybuf.at[0:15], y_s)
    for copy in row_rims[0] + row_rims[1] + [a9_copy] + b9_copies:
        copy.wait_send()
    drain(gwf.at[0:7], d_r)
    for tap in range(27):
        n, slot = (tap // 3, tap % 3) if tap < 24 else (tap - 24, 3)
        gw_ref[tap] = gwf[n, slot].astype(F32) * scale
    out_w = pltpu.make_async_copy(gw_ref, gw_hbm, io_sem.at[1])
    out_w.start()

    drain(gwf.at[0:7], d_s)
    out.wait()
    out_w.wait()


def hand_over(gi_in, gw_in, gi_out, gw_out, gi, gw, sems):
    pieces = [(gi_in.at[pl.ds(4 * n, 4)], gi.at[pl.ds(4 * n, 4)], gi_out.at[pl.ds(4 * n, 4)]) for n in range(4)]
    pieces.append((gw_in, gw, gw_out))
    loads = [pltpu.make_async_copy(src, mid, sems.at[0, n]) for n, (src, mid, _) in enumerate(pieces)]
    stores = [pltpu.make_async_copy(mid, dst, sems.at[1, n]) for n, (_, mid, dst) in enumerate(pieces)]
    for load in loads:
        load.start()
    for load, store in zip(loads, stores):
        load.wait()
        store.start()
    for store in stores:
        store.wait()


def body(inputs, filters, cotangent):
    cells = inputs.shape[1] * lax.axis_size("space") * inputs.shape[2] * inputs.shape[3]
    scale = 1.0 / math.sqrt(cells)
    sems = [0, 7, 0, 0, 0, 0, 0, 3, 0, 0, 2, 2, 8, 8, 0, 0, 0, 4, 0, 0, 0, 0, 3, 3, 0, 0, 0, 0, 3]
    scratch = [
        (inputs.shape, BF16),
        (filters.shape, BF16),
        (inputs.shape, BF16),
        (inputs.shape, BF16),
        (filters.shape, F32),
        ((PITCH * 16, 128), F32),
        ((34, 16, 512), BF16),
        ((32, 16, 512), BF16),
        ((32, 16, 128), BF16),
        ((6, 128, 768), BF16),
        ((4, 128, 512), BF16),
        ((32, 128, 128), BF16),
        ((384, 1152), BF16),
        ((384, 1152), BF16),
        ((4, 128, 512), F32),
        ((6, 768, 128), BF16),
        ((6, 128, 768), BF16),
        ((4, 384, 512), BF16),
        ((8, 3, 128, 128), F32),
        ((8, 3, 128, 128), BF16),
        ((4, 3, 128, 128), BF16),
        ((3, 3, 128, 128), BF16),
        ((3, 3, 128, 128), BF16),
        ((3, 128, 128), F32),
        ((3, 128, 128), BF16),
        ((3, 128, 128), BF16),
        ((3, 128, 128), BF16),
        ((3, 128, 128), BF16),
        ((4, 128, 128), BF16),
        ((16, 4, 16, 128), BF16),
        ((8, 4, 16, 128), BF16),
        ((4, 128, 512), BF16),
        ((32, 16, 512), BF16),
    ]
    hbm = pl.BlockSpec(memory_space=pl.ANY)
    grads = pl.pallas_call(
        lambda *refs: kernel(scale, *refs),
        out_shape=(
            jax.ShapeDtypeStruct(inputs.shape, BF16),
            jax.ShapeDtypeStruct(filters.shape, F32),
        ),
        in_specs=[hbm] * 3,
        out_specs=(hbm, hbm),
        scratch_shapes=[pltpu.VMEM(s, t) for s, t in scratch]
        + [pltpu.SemaphoreType.DMA((n,) if n else ()) for n in sems],
        compiler_params=pltpu.CompilerParams(
            collective_id=0, has_side_effects=True, vmem_limit_bytes=60 * 2**20
        ),
        name="conv_backward",
    )(inputs, filters, cotangent)
    return pl.pallas_call(
        hand_over,
        out_shape=tuple(jax.ShapeDtypeStruct(a.shape, a.dtype) for a in grads),
        in_specs=[hbm] * 2,
        out_specs=(hbm, hbm),
        scratch_shapes=[pltpu.VMEM(a.shape, a.dtype) for a in grads]
        + [pltpu.SemaphoreType.DMA((2, 5))],
        name="hand_over",
    )(*grads)


def solution(mesh):
    placed = (P("chan", "space", None, None), P(None, "chan", None), P("chan", "space", None, None))
    return jax.shard_map(
        body,
        mesh=mesh,
        in_specs=placed,
        out_specs=(P("chan", "space", None, None), P(None, "chan", None)),
        check_vma=False,
    )
```

```python
import math

import jax
import jax.numpy as jnp
from jax import lax
from jax.experimental import pallas as pl
from jax.experimental.pallas import tpu as pltpu
from jax.sharding import PartitionSpec as P

MESH = pl.DeviceIdType.MESH
BF16 = jnp.bfloat16
F32 = jnp.float32
PITCH = 136
STEPS = (2, 1, 3, 0)


def row_block(c):
    y = lax.div(c, 2)
    z = lax.rem(c, 2)
    q = lax.rem(y, 2)
    return 2 * y + z + q - 2 * z * q


class Copy:
    def __init__(self, src, dst, send_sem, recv_sem, where, sends=None, gets=None):
        self.copy = pltpu.make_async_remote_copy(
            src_ref=src, dst_ref=dst, send_sem=send_sem, recv_sem=recv_sem,
            device_id=where, device_id_type=MESH,
        )
        self.sends, self.gets = sends, gets

    def start(self):
        self.copy.start() if self.sends is None else pl.when(self.sends)(self.copy.start)
        return self

    def wait_recv(self):
        self.copy.wait_recv() if self.gets is None else pl.when(self.gets)(self.copy.wait_recv)

    def wait_send(self):
        self.copy.wait_send() if self.sends is None else pl.when(self.sends)(self.copy.wait_send)


def drain(like, sem, when=None):
    wait = pltpu.make_async_copy(like, like, sem).wait
    wait() if when is None else pl.when(when)(wait)


def shift_lanes(block, by):
    lane = lax.broadcasted_iota(jnp.int32, (block.shape[0], 128), 1)
    edge = 0 if by == 1 else 127
    pieces = []
    for d in range(block.shape[1] // 128):
        rolled = pltpu.roll(block[:, 128 * d : 128 * d + 128], by % 128, 1)
        pieces.append(jnp.where(lane == edge, 0.0, rolled))
    return jnp.concatenate(pieces, axis=1)


def kernel(
    scale, x_hbm, f_hbm, t_hbm, gi_hbm, gw_hbm,
    x_ref, f_ref, t_ref, gi_ref, gw_ref, wide, xt, tt, fp, xb, ct, wall, wg, wf, pre, xtt, gb, gs, gw, gwb, abuf, sb, xbuf,
    gw9, gwb9, abuf9, sb9, xbuf9, yb, ybuf, gwf,
    gout, back,
    x_s, x_r, t_s, t_r, wy_s, wy_r, wx_s, wx_r, wd_s, wd_r, xh_s, xh_r, gh_s, gh_r, gi_s, gi_r,
    a_s, a_r, a9_s, a9_r, b_s, b_r, b9_s, b9_r, y_s, y_r, d_s, d_r, io_sem,
):
    c = lax.axis_index("chan")
    g = lax.axis_index("space")
    r = row_block(c)
    core = lax.rem(g, 2)
    px = lax.rem(lax.div(g, 2), 4)
    pz = lax.div(g, 8)
    sibling = g + 1 - 2 * core
    mine = pl.ds(pl.multiple_of(16 * c, 16), 16)
    has_lo, has_hi = g > 0, g < 15
    has_up, has_down = r > 0, r < 7

    def chan_peer(k):
        return lax.rem(c + k, 8)

    def x_peer(k):
        return 8 * pz + 2 * lax.rem(px + k, 4) + core

    def half_peer(k):
        return 8 * pz + lax.rem(2 * px + core + k, 8)

    barrier = pltpu.get_barrier_semaphore()
    for k in range(1, 8):
        pl.semaphore_signal(barrier, inc=1, device_id={"chan": chan_peer(k)}, device_id_type=MESH)
    for k in range(1, 8):
        pl.semaphore_signal(barrier, inc=1, device_id={"space": half_peer(k)}, device_id_type=MESH)
    for k in range(8):
        pl.semaphore_signal(
            barrier, inc=1, device_id={"space": lax.rem(g + 8, 16), "chan": chan_peer(k)},
            device_id_type=MESH,
        )
    for edge, dg in ((7, 1), (8, -1)):

        @pl.when(g == edge)
        def _():
            pl.semaphore_signal(barrier, inc=1, device_id={"space": g + dg}, device_id_type=MESH)

    for dg, has_g in ((-1, has_lo), (1, has_hi)):
        for dr, has_r in ((-1, has_up), (1, has_down)):

            @pl.when(jnp.logical_and(has_g, has_r))
            def _():
                pl.semaphore_signal(
                    barrier, inc=1,
                    device_id={"space": g + dg, "chan": row_block(r + dr)}, device_id_type=MESH,
                )

    loads = [
        pltpu.make_async_copy(src, dst, io_sem.at[n])
        for n, (src, dst) in enumerate(((x_hbm, x_ref), (f_hbm, f_ref), (t_hbm, t_ref)))
    ]
    for load in loads:
        load.start()

    xt[0] = jnp.zeros((16, 512), BF16)
    xt[33] = jnp.zeros((16, 512), BF16)

    @pl.when(g == 0)
    def _():
        xb[:, :, 0:128] = jnp.zeros((6, 128, 128), BF16)
        gb[:, :, 0:128] = jnp.zeros((6, 128, 128), BF16)

    @pl.when(g == 15)
    def _():
        xb[:, :, 640:768] = jnp.zeros((6, 128, 128), BF16)
        gb[:, :, 640:768] = jnp.zeros((6, 128, 128), BF16)

    @pl.when(r == 0)
    def _():
        gb[0] = jnp.zeros((128, 768), BF16)

    @pl.when(r == 7)
    def _():
        gb[5] = jnp.zeros((128, 768), BF16)


    def to_rows(src, dst, first):
        for ch in range(16):
            wide[PITCH * ch : PITCH * ch + 128, :] = src[ch].reshape(128, 128).astype(F32)

        def step(h, _):
            for d in range(4):
                rows = wide[pl.ds(32 * d + h, 16, stride=PITCH), :]
                dst[first + h, :, 128 * d : 128 * d + 128] = rows.astype(BF16)
            return 0

        lax.fori_loop(0, 32, step, 0)

    loads[0].wait()
    to_rows(x_ref, xt, 1)
    sides_g = has_lo.astype(jnp.int32) + has_hi.astype(jnp.int32)
    sides_r = has_up.astype(jnp.int32) + has_down.astype(jnp.int32)
    middle = (g == 7).astype(jnp.int32) + (g == 8).astype(jnp.int32)
    loads[1].wait()
    fp[0:27] = f_ref[...]
    fp[27:32] = jnp.zeros((5, 16, 128), BF16)
    pl.semaphore_wait(barrier, 22 + middle + sides_g * sides_r)

    part = 4 * (4 * core + px)
    some = part < 28
    wy_copies = [
        Copy(
            fp.at[pl.ds(part, 4)], wall.at[pl.ds(part, 4), mine, :],
            wy_s, wy_r, {"chan": chan_peer(k)}, some, some,
        ).start()
        for k in range(1, 8)
    ]
    wall[pl.ds(part, 4), mine, :] = fp[pl.ds(part, 4)]
    x_copies = [
        Copy(
            xt.at[pl.ds(4 * row_block(chan_peer(k)), 6)], xb.at[:, mine, 128:640],
            x_s, x_r.at[k - 1], {"chan": chan_peer(k)},
        ).start()
        for k in range(1, 8)
    ]
    xb[:, mine, 128:640] = xt[pl.ds(4 * r, 6)]
    loads[2].wait()
    to_rows(t_ref, tt, 0)
    t_copies = [
        Copy(
            tt.at[pl.ds(4 * row_block(chan_peer(k)), 4)], ct.at[:, mine, :],
            t_s, t_r, {"chan": chan_peer(k)},
        ).start()
        for k in range(1, 8)
    ]
    ct[:, mine, :] = tt[pl.ds(4 * r, 4)]
    drain(fp.at[0:28], wy_r, some)
    wx_copies = [
        Copy(
            wall.at[pl.ds(part, 4)], wall.at[pl.ds(part, 4)],
            wx_s, wx_r.at[k - 1], {"space": x_peer(k)},
            some, core + lax.rem(px + 4 - k, 4) < 4,
        ).start()
        for k in range(1, 4)
    ]

    wd_copies = []

    def pass_filters(k):
        owner = lax.rem(px + 4 - k, 4)
        piece = wall.at[pl.ds(4 * (4 * core + owner), 4)]
        wd_copies.append(Copy(
            piece, piece, wd_s, wd_r, {"space": sibling},
            core + owner < 4, 1 - core + owner < 4,
        ).start())

    pass_filters(0)

    h_copies = []

    def pass_rims(k):
        rows = pl.ds(pl.multiple_of(16 * lax.rem(c + 8 - k, 8), 16), 16)
        for n, at, to, dg in ((0, 128, 640, -1), (1, 512, 0, 1)):
            has_g, from_g = (has_lo, has_hi) if dg < 0 else (has_hi, has_lo)
            h_copies.append(Copy(
                xb.at[:, rows, at : at + 128], xb.at[:, rows, to : to + 128],
                xh_s.at[n], xh_r.at[n], {"space": g + dg}, has_g, from_g,
            ).start())

    pass_rims(0)
    for k in range(1, 6):
        x_copies[k - 1].wait_recv()
        pass_rims(k)
    for k in range(1, 4):
        wx_copies[k - 1].wait_recv()
        pass_filters(k)
    for k in range(6, 8):
        x_copies[k - 1].wait_recv()
        pass_rims(k)
    drain(wall.at[0:12], wd_r, core == 0)
    drain(wall.at[0:16], wd_r, core == 1)
    for tap in range(27):
        a, b, cc = tap // 9, tap // 3 % 3, tap % 3
        block = wall[tap]
        rows = slice(128 * cc, 128 * cc + 128)
        wg[rows, 128 * (8 - 3 * a - b) : 128 * (9 - 3 * a - b)] = block
        wf[rows, 128 * (3 * a + b) : 128 * (3 * a + b + 1)] = block.T
    drain(xb.at[:, :, 640:768], xh_r.at[0], has_hi)
    drain(xb.at[:, :, 0:128], xh_r.at[1], has_lo)

    def patches(src, h):
        rows = [src[h + b, :, 128 * a : 128 * a + 512] for a in range(3) for b in range(3)]
        return jnp.concatenate(rows, axis=0)

    def forward(h, _):
        acc = jnp.dot(wf[...], patches(xb, h), preferred_element_type=F32)
        pre[h] = shift_lanes(acc[0:128], 1) + acc[128:256] + shift_lanes(acc[256:384], -1)
        for n in range(9):
            row, plane = lax.div(9 * h + n, 6), lax.rem(9 * h + n, 6)
            at = pl.ds(pl.multiple_of(128 * plane, 128), 128)
            xtt[row, at, :] = xb[row, :, at].T
        return 0

    lax.fori_loop(0, 4, forward, 0)
    drain(ct.at[:, 0:112, :], t_r)

    up, down = row_block(lax.max(r - 1, 0)), row_block(lax.min(r + 1, 7))
    row_rims, plane_rims = [], []

    def send_rims(row, to_row, has_r, from_r, to):
        n = 3 * len(row_rims)
        sent = [Copy(
            gb.at[row, :, 128:640], gb.at[to_row, :, 128:640], gh_s.at[n], gh_r.at[n],
            {"chan": to}, has_r, from_r,
        ).start()]
        for m, plane, to_plane, dg in ((1, 128, 640, -1), (2, 512, 0, 1)):
            has_g, from_g = (has_lo, has_hi) if dg < 0 else (has_hi, has_lo)
            sent.append(Copy(
                gb.at[row, :, plane : plane + 128], gb.at[to_row, :, to_plane : to_plane + 128],
                gh_s.at[n + m], gh_r.at[n + m], {"space": g + dg, "chan": to},
                jnp.logical_and(has_g, has_r), jnp.logical_and(from_g, from_r),
            ).start())
        row_rims.append(sent)

    for h in (0, 3, 1, 2):
        p = pre[h]
        sigma = 1.0 / (1.0 + jnp.exp(-p))
        grad = ct[h].astype(F32) * sigma * (1.0 + p * (1.0 - sigma))
        gb[h + 1, :, 128:640] = grad.astype(BF16)
        for n, at, to, dg in ((6, 128, 640, -1), (7, 512, 0, 1)):
            has_g, from_g = (has_lo, has_hi) if dg < 0 else (has_hi, has_lo)
            plane_rims.append(Copy(
                gb.at[h + 1, :, at : at + 128], gb.at[h + 1, :, to : to + 128],
                gh_s.at[n], gh_r.at[n], {"space": g + dg}, has_g, from_g,
            ).start())
        if h == 0:
            send_rims(1, 5, has_up, has_down, up)
        if h == 3:
            send_rims(4, 0, has_down, has_up, down)
        gs[h, 0:128, :] = shift_lanes(grad, -1).astype(BF16)
        gs[h, 128:256, :] = grad.astype(BF16)
        gs[h, 256:384, :] = shift_lanes(grad, 1).astype(BF16)

    grads = jnp.concatenate([gs[h] for h in range(4)], axis=1)

    def product(*offsets):
        sides = []
        for ab in offsets:
            lanes = pl.ds(pl.multiple_of(128 * lax.div(ab, 3), 128), 512)
            rows = [xtt[h + lax.rem(ab, 3), lanes, :] for h in range(4)]
            sides.append(jnp.concatenate(rows, axis=0))
        side = sides[0] if len(sides) == 1 else jnp.concatenate(sides, axis=1)
        return jnp.dot(grads, side, preferred_element_type=F32)

    a_copies, b_copies = [], []
    first = core == 0

    def pair_sum(j):
        a_copies[j].wait_recv()
        q = lax.rem(px + STEPS[j], 4)
        total = gw[4 * core + q] + abuf[j].astype(F32)
        if STEPS[j] == 0:
            return total
        sb[j] = total.astype(BF16)
        b_copies.append(Copy(
            sb.at[j], xbuf.at[j], b_s, b_r, {"space": x_peer(STEPS[j])}
        ).start())

    for j in range(4):
        q = lax.rem(px + STEPS[j], 4)
        prod = product(q, q + 4)
        for cc in range(3):
            for n in range(2):
                block = prod[128 * cc : 128 * cc + 128, 128 * n : 128 * n + 128]
                gw[4 * n + q, cc] = block
                gwb[4 * n + q, cc] = block.astype(BF16)
        a_copies.append(Copy(
            gwb.at[4 * (1 - core) + q], abuf.at[j], a_s, a_r.at[j], {"space": sibling}
        ).start())
        if j == 1:
            ninth = product(jnp.int32(8))
            for n in range(3):
                gw9[n] = ninth[128 * n : 128 * n + 128]
                gwb9[n] = ninth[128 * n : 128 * n + 128].astype(BF16)
            a9_copy = Copy(
                gwb9, abuf9, a9_s, a9_r, {"space": sibling}, core == 1, first
            ).start()
        if j:
            pair_sum(j - 1)
    a9_copy.wait_recv()

    @pl.when(first)
    def _():
        gw9[...] = gw9[...] + abuf9[...].astype(F32)
        sb9[...] = gw9[...].astype(BF16)

    b9_copies = []
    for k in range(1, 4):
        q = lax.rem(px + k, 4)
        b9_copies.append(Copy(
            sb9.at[lax.min(q, 2)], xbuf9.at[k - 1], b9_s.at[k - 1], b9_r.at[k - 1],
            {"space": x_peer(k)}, jnp.logical_and(first, q < 3), jnp.logical_and(first, px < 3),
        ).start())

    gi_copies = []

    def backward(h):
        acc = jnp.dot(wg[...], patches(gb, h), preferred_element_type=F32)
        total = shift_lanes(acc[0:128], -1) + acc[128:256] + shift_lanes(acc[256:384], 1)
        gout[h] = total.astype(BF16)

    def send_rows(first, count):
        for k in range(1, 8):
            to = pl.ds(pl.multiple_of(16 * chan_peer(k), 16), 16)
            gi_copies.append(Copy(
                gout.at[pl.ds(first, count), to, :], back.at[pl.ds(4 * r + first, count)],
                gi_s, gi_r, {"chan": chan_peer(k)},
            ).start())
        back[pl.ds(4 * r + first, count)] = gout[first : first + count, mine, :]

    def finish_rows():
        drain(gb.at[1:5, :, 640:768], gh_r.at[6], has_hi)
        drain(gb.at[1:5, :, 0:128], gh_r.at[7], has_lo)
        backward(1)
        backward(2)
        send_rows(1, 2)
        for sent in row_rims:
            for copy in sent:
                copy.wait_recv()
        backward(0)
        backward(3)

    late = g == 8
    pl.when(jnp.logical_not(late))(finish_rows)

    total = pair_sum(3)
    drain(xbuf, b_r)
    for j in range(3):
        total = total + xbuf[j].astype(F32)
    for slot in range(3):
        yb[slot] = total[slot].T.astype(BF16)
    yb[3] = jnp.zeros((128, 128), BF16)
    for copy in b9_copies:
        copy.wait_recv()

    @pl.when(jnp.logical_and(first, px < 3))
    def _():
        total9 = gw9[lax.min(px, 2)]
        for j in range(3):
            total9 = total9 + xbuf9[j].astype(F32)
        yb[3] = total9.T.astype(BF16)

    y_copies = []
    for dz in range(2):
        for k in range(8):
            if dz or k:
                z, to = lax.rem(pz + dz, 2), chan_peer(k)
                y_copies.append(Copy(
                    yb.at[:, pl.ds(pl.multiple_of(16 * to, 16), 16), :], ybuf.at[8 * pz + c],
                    y_s, y_r, {"space": 8 * z + 2 * px + core, "chan": to},
                ).start())
    ybuf[8 * pz + c] = yb[:, mine, :]
    pl.when(late)(finish_rows)
    send_rows(0, 1)
    send_rows(3, 1)
    drain(ybuf.at[0:15], y_r)
    total = ybuf[0].astype(F32)
    for n in range(1, 16):
        total = total + ybuf[n].astype(F32)
    piece = gwf.at[4 * core + px]
    piece[...] = total.astype(BF16)
    d_copies = [
        Copy(piece, piece, d_s, d_r, {"space": half_peer(k)}).start()
        for k in range(1, 8)
    ]
    drain(back.at[0:28], gi_r)
    for d in range(4):
        for h in range(32):
            wide[24 * h : 24 * h + 16, :] = back[h, :, 128 * d : 128 * d + 128].astype(F32)

        def step(ch, _):
            gi_ref[ch, d] = wide[pl.ds(ch, 32, stride=24), :].astype(BF16)
            return 0

        lax.fori_loop(0, 16, step, 0)
    out = pltpu.make_async_copy(gi_ref, gi_hbm, io_sem.at[0])
    out.start()
    drain(fp.at[0:28], wy_s, some)
    drain(xb.at[:, 0:112, 128:640], x_s)
    drain(ct.at[:, 0:112, :], t_s)
    drain(wall.at[0:12], wx_s, some)
    drain(wall.at[0:16], wd_s, core == 0)
    drain(wall.at[0:12], wd_s, core == 1)
    drain(xb.at[:, :, 128:256], xh_s.at[0], has_lo)
    drain(xb.at[:, :, 512:640], xh_s.at[1], has_hi)
    drain(gb.at[1:5, :, 128:256], gh_s.at[6], has_lo)
    drain(gb.at[1:5, :, 512:640], gh_s.at[7], has_hi)
    drain(back.at[0:28], gi_s)
    drain(gwb.at[0:4], a_s)
    drain(sb, b_s)
    drain(ybuf.at[0:15], y_s)
    for copy in row_rims[0] + row_rims[1] + [a9_copy] + b9_copies:
        copy.wait_send()
    drain(gwf.at[0:7], d_r)
    for tap in range(27):
        n, slot = (tap // 3, tap % 3) if tap < 24 else (tap - 24, 3)
        gw_ref[tap] = gwf[n, slot].astype(F32) * scale
    out_w = pltpu.make_async_copy(gw_ref, gw_hbm, io_sem.at[1])
    out_w.start()

    drain(gwf.at[0:7], d_s)
    out.wait()
    out_w.wait()


def hand_over(gi_in, gw_in, gi_out, gw_out, gi, gw, sems):
    pieces = [(gi_in.at[pl.ds(4 * n, 4)], gi.at[pl.ds(4 * n, 4)], gi_out.at[pl.ds(4 * n, 4)]) for n in range(4)]
    pieces.append((gw_in, gw, gw_out))
    loads = [pltpu.make_async_copy(src, mid, sems.at[0, n]) for n, (src, mid, _) in enumerate(pieces)]
    stores = [pltpu.make_async_copy(mid, dst, sems.at[1, n]) for n, (_, mid, dst) in enumerate(pieces)]
    for load in loads:
        load.start()
    for load, store in zip(loads, stores):
        load.wait()
        store.start()
    for store in stores:
        store.wait()


def body(inputs, filters, cotangent):
    cells = inputs.shape[1] * lax.axis_size("space") * inputs.shape[2] * inputs.shape[3]
    scale = 1.0 / math.sqrt(cells)
    sems = [0, 7, 0, 0, 0, 0, 0, 3, 0, 0, 2, 2, 8, 8, 0, 0, 0, 4, 0, 0, 0, 0, 3, 3, 0, 0, 0, 0, 3]
    scratch = [
        (inputs.shape, BF16),
        (filters.shape, BF16),
        (inputs.shape, BF16),
        (inputs.shape, BF16),
        (filters.shape, F32),
        ((PITCH * 16, 128), F32),
        ((34, 16, 512), BF16),
        ((32, 16, 512), BF16),
        ((32, 16, 128), BF16),
        ((6, 128, 768), BF16),
        ((4, 128, 512), BF16),
        ((32, 128, 128), BF16),
        ((384, 1152), BF16),
        ((384, 1152), BF16),
        ((4, 128, 512), F32),
        ((6, 768, 128), BF16),
        ((6, 128, 768), BF16),
        ((4, 384, 512), BF16),
        ((8, 3, 128, 128), F32),
        ((8, 3, 128, 128), BF16),
        ((4, 3, 128, 128), BF16),
        ((3, 3, 128, 128), BF16),
        ((3, 3, 128, 128), BF16),
        ((3, 128, 128), F32),
        ((3, 128, 128), BF16),
        ((3, 128, 128), BF16),
        ((3, 128, 128), BF16),
        ((3, 128, 128), BF16),
        ((4, 128, 128), BF16),
        ((16, 4, 16, 128), BF16),
        ((8, 4, 16, 128), BF16),
        ((4, 128, 512), BF16),
        ((32, 16, 512), BF16),
    ]
    hbm = pl.BlockSpec(memory_space=pl.ANY)
    grads = pl.pallas_call(
        lambda *refs: kernel(scale, *refs),
        out_shape=(
            jax.ShapeDtypeStruct(inputs.shape, BF16),
            jax.ShapeDtypeStruct(filters.shape, F32),
        ),
        in_specs=[hbm] * 3,
        out_specs=(hbm, hbm),
        scratch_shapes=[pltpu.VMEM(s, t) for s, t in scratch]
        + [pltpu.SemaphoreType.DMA((n,) if n else ()) for n in sems],
        compiler_params=pltpu.CompilerParams(
            collective_id=0, has_side_effects=True, vmem_limit_bytes=60 * 2**20
        ),
        name="conv_backward",
    )(inputs, filters, cotangent)
    return pl.pallas_call(
        hand_over,
        out_shape=tuple(jax.ShapeDtypeStruct(a.shape, a.dtype) for a in grads),
        in_specs=[hbm] * 2,
        out_specs=(hbm, hbm),
        scratch_shapes=[pltpu.VMEM(a.shape, a.dtype) for a in grads]
        + [pltpu.SemaphoreType.DMA((2, 5))],
        name="hand_over",
    )(*grads)


def solution(mesh):
    placed = (P("chan", "space", None, None), P(None, "chan", None), P("chan", "space", None, None))
    return jax.shard_map(
        body,
        mesh=mesh,
        in_specs=placed,
        out_specs=(P("chan", "space", None, None), P(None, "chan", None)),
        check_vma=False,
    )
```

```python
import math

import jax
import jax.numpy as jnp
from jax import lax
from jax.experimental import pallas as pl
from jax.experimental.pallas import tpu as pltpu
from jax.sharding import PartitionSpec as P

MESH = pl.DeviceIdType.MESH
BF16 = jnp.bfloat16
F32 = jnp.float32
PITCH = 136
STEPS = (2, 1, 3, 0)


def row_block(c):
    y = lax.div(c, 2)
    z = lax.rem(c, 2)
    q = lax.rem(y, 2)
    return 2 * y + z + q - 2 * z * q


class Copy:
    def __init__(self, src, dst, send_sem, recv_sem, where, sends=None, gets=None):
        self.copy = pltpu.make_async_remote_copy(
            src_ref=src, dst_ref=dst, send_sem=send_sem, recv_sem=recv_sem,
            device_id=where, device_id_type=MESH,
        )
        self.sends, self.gets = sends, gets

    def start(self):
        self.copy.start() if self.sends is None else pl.when(self.sends)(self.copy.start)
        return self

    def wait_recv(self):
        self.copy.wait_recv() if self.gets is None else pl.when(self.gets)(self.copy.wait_recv)

    def wait_send(self):
        self.copy.wait_send() if self.sends is None else pl.when(self.sends)(self.copy.wait_send)


def drain(like, sem, when=None):
    wait = pltpu.make_async_copy(like, like, sem).wait
    wait() if when is None else pl.when(when)(wait)


def shift_lanes(block, by):
    lane = lax.broadcasted_iota(jnp.int32, (block.shape[0], 128), 1)
    edge = 0 if by == 1 else 127
    pieces = []
    for d in range(block.shape[1] // 128):
        rolled = pltpu.roll(block[:, 128 * d : 128 * d + 128], by % 128, 1)
        pieces.append(jnp.where(lane == edge, 0.0, rolled))
    return jnp.concatenate(pieces, axis=1)


def kernel(
    scale, x_hbm, f_hbm, t_hbm, gi_hbm, gw_hbm,
    x_ref, f_ref, t_ref, gi_ref, gw_ref, wide, xt, tt, fp, xb, ct, wall, wg, wf, pre, xtt, gb, gs, gw, gwb, abuf, sb, xbuf,
    gw9, gwb9, abuf9, sb9, xbuf9, yb, ybuf, gwf,
    gout, back,
    x_s, x_r, t_s, t_r, wy_s, wy_r, wx_s, wx_r, wd_s, wd_r, xh_s, xh_r, gh_s, gh_r, gi_s, gi_r,
    a_s, a_r, a9_s, a9_r, b_s, b_r, b9_s, b9_r, y_s, y_r, d_s, d_r, io_sem,
):
    c = lax.axis_index("chan")
    g = lax.axis_index("space")
    r = row_block(c)
    core = lax.rem(g, 2)
    px = lax.rem(lax.div(g, 2), 4)
    pz = lax.div(g, 8)
    sibling = g + 1 - 2 * core
    mine = pl.ds(pl.multiple_of(16 * c, 16), 16)
    has_lo, has_hi = g > 0, g < 15
    has_up, has_down = r > 0, r < 7

    def chan_peer(k):
        return lax.rem(c + k, 8)

    def x_peer(k):
        return 8 * pz + 2 * lax.rem(px + k, 4) + core

    def half_peer(k):
        return 8 * pz + lax.rem(2 * px + core + k, 8)

    barrier = pltpu.get_barrier_semaphore()
    for k in range(1, 8):
        pl.semaphore_signal(barrier, inc=1, device_id={"chan": chan_peer(k)}, device_id_type=MESH)
    for k in range(1, 8):
        pl.semaphore_signal(barrier, inc=1, device_id={"space": half_peer(k)}, device_id_type=MESH)
    for k in range(8):
        pl.semaphore_signal(
            barrier, inc=1, device_id={"space": lax.rem(g + 8, 16), "chan": chan_peer(k)},
            device_id_type=MESH,
        )
    for edge, dg in ((7, 1), (8, -1)):

        @pl.when(g == edge)
        def _():
            pl.semaphore_signal(barrier, inc=1, device_id={"space": g + dg}, device_id_type=MESH)

    for dg, has_g in ((-1, has_lo), (1, has_hi)):
        for dr, has_r in ((-1, has_up), (1, has_down)):

            @pl.when(jnp.logical_and(has_g, has_r))
            def _():
                pl.semaphore_signal(
                    barrier, inc=1,
                    device_id={"space": g + dg, "chan": row_block(r + dr)}, device_id_type=MESH,
                )

    loads = [
        pltpu.make_async_copy(src, dst, io_sem.at[n])
        for n, (src, dst) in enumerate(((x_hbm, x_ref), (f_hbm, f_ref), (t_hbm, t_ref)))
    ]
    for load in loads:
        load.start()

    xt[0] = jnp.zeros((16, 512), BF16)
    xt[33] = jnp.zeros((16, 512), BF16)

    @pl.when(g == 0)
    def _():
        xb[:, :, 0:128] = jnp.zeros((6, 128, 128), BF16)
        gb[:, :, 0:128] = jnp.zeros((6, 128, 128), BF16)

    @pl.when(g == 15)
    def _():
        xb[:, :, 640:768] = jnp.zeros((6, 128, 128), BF16)
        gb[:, :, 640:768] = jnp.zeros((6, 128, 128), BF16)

    @pl.when(r == 0)
    def _():
        gb[0] = jnp.zeros((128, 768), BF16)

    @pl.when(r == 7)
    def _():
        gb[5] = jnp.zeros((128, 768), BF16)


    def to_rows(src, dst, first):
        for ch in range(16):
            wide[PITCH * ch : PITCH * ch + 128, :] = src[ch].reshape(128, 128).astype(F32)

        def step(h, _):
            for d in range(4):
                rows = wide[pl.ds(32 * d + h, 16, stride=PITCH), :]
                dst[first + h, :, 128 * d : 128 * d + 128] = rows.astype(BF16)
            return 0

        lax.fori_loop(0, 32, step, 0)

    loads[0].wait()
    to_rows(x_ref, xt, 1)
    sides_g = has_lo.astype(jnp.int32) + has_hi.astype(jnp.int32)
    sides_r = has_up.astype(jnp.int32) + has_down.astype(jnp.int32)
    middle = (g == 7).astype(jnp.int32) + (g == 8).astype(jnp.int32)
    loads[1].wait()
    fp[0:27] = f_ref[...]
    fp[27:32] = jnp.zeros((5, 16, 128), BF16)
    pl.semaphore_wait(barrier, 22 + middle + sides_g * sides_r)

    part = 4 * (4 * core + px)
    some = part < 28
    wy_copies = [
        Copy(
            fp.at[pl.ds(part, 4)], wall.at[pl.ds(part, 4), mine, :],
            wy_s, wy_r, {"chan": chan_peer(k)}, some, some,
        ).start()
        for k in range(1, 8)
    ]
    wall[pl.ds(part, 4), mine, :] = fp[pl.ds(part, 4)]
    x_copies = [
        Copy(
            xt.at[pl.ds(4 * row_block(chan_peer(k)), 6)], xb.at[:, mine, 128:640],
            x_s, x_r.at[k - 1], {"chan": chan_peer(k)},
        ).start()
        for k in range(1, 8)
    ]
    xb[:, mine, 128:640] = xt[pl.ds(4 * r, 6)]
    loads[2].wait()
    to_rows(t_ref, tt, 0)
    t_copies = [
        Copy(
            tt.at[pl.ds(4 * row_block(chan_peer(k)), 4)], ct.at[:, mine, :],
            t_s, t_r, {"chan": chan_peer(k)},
        ).start()
        for k in range(1, 8)
    ]
    ct[:, mine, :] = tt[pl.ds(4 * r, 4)]
    drain(fp.at[0:28], wy_r, some)
    wx_copies = [
        Copy(
            wall.at[pl.ds(part, 4)], wall.at[pl.ds(part, 4)],
            wx_s, wx_r.at[k - 1], {"space": x_peer(k)},
            some, core + lax.rem(px + 4 - k, 4) < 4,
        ).start()
        for k in range(1, 4)
    ]

    wd_copies = []

    def pass_filters(k):
        owner = lax.rem(px + 4 - k, 4)
        piece = wall.at[pl.ds(4 * (4 * core + owner), 4)]
        wd_copies.append(Copy(
            piece, piece, wd_s, wd_r, {"space": sibling},
            core + owner < 4, 1 - core + owner < 4,
        ).start())

    pass_filters(0)

    h_copies = []

    def pass_rims(k):
        rows = pl.ds(pl.multiple_of(16 * lax.rem(c + 8 - k, 8), 16), 16)
        for n, at, to, dg in ((0, 128, 640, -1), (1, 512, 0, 1)):
            has_g, from_g = (has_lo, has_hi) if dg < 0 else (has_hi, has_lo)
            h_copies.append(Copy(
                xb.at[:, rows, at : at + 128], xb.at[:, rows, to : to + 128],
                xh_s.at[n], xh_r.at[n], {"space": g + dg}, has_g, from_g,
            ).start())

    pass_rims(0)
    for k in range(1, 6):
        x_copies[k - 1].wait_recv()
        pass_rims(k)
    for k in range(1, 4):
        wx_copies[k - 1].wait_recv()
        pass_filters(k)
    for k in range(6, 8):
        x_copies[k - 1].wait_recv()
        pass_rims(k)
    drain(wall.at[0:12], wd_r, core == 0)
    drain(wall.at[0:16], wd_r, core == 1)
    for tap in range(27):
        a, b, cc = tap // 9, tap // 3 % 3, tap % 3
        block = wall[tap]
        rows = slice(128 * cc, 128 * cc + 128)
        wg[rows, 128 * (8 - 3 * a - b) : 128 * (9 - 3 * a - b)] = block
        wf[rows, 128 * (3 * a + b) : 128 * (3 * a + b + 1)] = block.T

    def patches(src, h, offsets=(0, 1, 2)):
        rows = [src[h + b, :, 128 * a : 128 * a + 512] for a in offsets for b in range(3)]
        return jnp.concatenate(rows, axis=0)

    def centre(h, _):
        acc = jnp.dot(wf[:, 384:768], patches(xb, h, (1,)), preferred_element_type=F32)
        pre[h] = shift_lanes(acc[0:128], 1) + acc[128:256] + shift_lanes(acc[256:384], -1)
        return 0

    lax.fori_loop(0, 4, centre, 0)
    drain(xb.at[:, :, 640:768], xh_r.at[0], has_hi)
    drain(xb.at[:, :, 0:128], xh_r.at[1], has_lo)

    def forward(h, _):
        sides = jnp.concatenate([wf[:, 0:384], wf[:, 768:1152]], axis=1)
        acc = jnp.dot(sides, patches(xb, h, (0, 2)), preferred_element_type=F32)
        pre[h] = pre[h] + shift_lanes(acc[0:128], 1) + acc[128:256] + shift_lanes(acc[256:384], -1)
        for n in range(9):
            row, plane = lax.div(9 * h + n, 6), lax.rem(9 * h + n, 6)
            at = pl.ds(pl.multiple_of(128 * plane, 128), 128)
            xtt[row, at, :] = xb[row, :, at].T
        return 0

    lax.fori_loop(0, 4, forward, 0)
    drain(ct.at[:, 0:112, :], t_r)

    up, down = row_block(lax.max(r - 1, 0)), row_block(lax.min(r + 1, 7))
    row_rims, plane_rims = [], []

    def send_rims(row, to_row, has_r, from_r, to):
        n = 3 * len(row_rims)
        sent = [Copy(
            gb.at[row, :, 128:640], gb.at[to_row, :, 128:640], gh_s.at[n], gh_r.at[n],
            {"chan": to}, has_r, from_r,
        ).start()]
        for m, plane, to_plane, dg in ((1, 128, 640, -1), (2, 512, 0, 1)):
            has_g, from_g = (has_lo, has_hi) if dg < 0 else (has_hi, has_lo)
            sent.append(Copy(
                gb.at[row, :, plane : plane + 128], gb.at[to_row, :, to_plane : to_plane + 128],
                gh_s.at[n + m], gh_r.at[n + m], {"space": g + dg, "chan": to},
                jnp.logical_and(has_g, has_r), jnp.logical_and(from_g, from_r),
            ).start())
        row_rims.append(sent)

    for h in (0, 3, 1, 2):
        p = pre[h]
        sigma = 1.0 / (1.0 + jnp.exp(-p))
        grad = ct[h].astype(F32) * sigma * (1.0 + p * (1.0 - sigma))
        gb[h + 1, :, 128:640] = grad.astype(BF16)
        for n, at, to, dg in ((6, 128, 640, -1), (7, 512, 0, 1)):
            has_g, from_g = (has_lo, has_hi) if dg < 0 else (has_hi, has_lo)
            plane_rims.append(Copy(
                gb.at[h + 1, :, at : at + 128], gb.at[h + 1, :, to : to + 128],
                gh_s.at[n], gh_r.at[n], {"space": g + dg}, has_g, from_g,
            ).start())
        if h == 0:
            send_rims(1, 5, has_up, has_down, up)
        if h == 3:
            send_rims(4, 0, has_down, has_up, down)
        gs[h, 0:128, :] = shift_lanes(grad, -1).astype(BF16)
        gs[h, 128:256, :] = grad.astype(BF16)
        gs[h, 256:384, :] = shift_lanes(grad, 1).astype(BF16)

    grads = jnp.concatenate([gs[h] for h in range(4)], axis=1)

    def product(*offsets):
        sides = []
        for ab in offsets:
            lanes = pl.ds(pl.multiple_of(128 * lax.div(ab, 3), 128), 512)
            rows = [xtt[h + lax.rem(ab, 3), lanes, :] for h in range(4)]
            sides.append(jnp.concatenate(rows, axis=0))
        side = sides[0] if len(sides) == 1 else jnp.concatenate(sides, axis=1)
        return jnp.dot(grads, side, preferred_element_type=F32)

    a_copies, b_copies = [], []
    first = core == 0

    def pair_sum(j):
        a_copies[j].wait_recv()
        q = lax.rem(px + STEPS[j], 4)
        total = gw[4 * core + q] + abuf[j].astype(F32)
        if STEPS[j] == 0:
            return total
        sb[j] = total.astype(BF16)
        b_copies.append(Copy(
            sb.at[j], xbuf.at[j], b_s, b_r, {"space": x_peer(STEPS[j])}
        ).start())

    for j in range(4):
        q = lax.rem(px + STEPS[j], 4)
        prod = product(q, q + 4)
        for cc in range(3):
            for n in range(2):
                block = prod[128 * cc : 128 * cc + 128, 128 * n : 128 * n + 128]
                gw[4 * n + q, cc] = block
                gwb[4 * n + q, cc] = block.astype(BF16)
        a_copies.append(Copy(
            gwb.at[4 * (1 - core) + q], abuf.at[j], a_s, a_r.at[j], {"space": sibling}
        ).start())
        if j == 1:
            ninth = product(jnp.int32(8))
            for n in range(3):
                gw9[n] = ninth[128 * n : 128 * n + 128]
                gwb9[n] = ninth[128 * n : 128 * n + 128].astype(BF16)
            a9_copy = Copy(
                gwb9, abuf9, a9_s, a9_r, {"space": sibling}, core == 1, first
            ).start()
        if j:
            pair_sum(j - 1)
    a9_copy.wait_recv()

    @pl.when(first)
    def _():
        gw9[...] = gw9[...] + abuf9[...].astype(F32)
        sb9[...] = gw9[...].astype(BF16)

    b9_copies = []
    for k in range(1, 4):
        q = lax.rem(px + k, 4)
        b9_copies.append(Copy(
            sb9.at[lax.min(q, 2)], xbuf9.at[k - 1], b9_s.at[k - 1], b9_r.at[k - 1],
            {"space": x_peer(k)}, jnp.logical_and(first, q < 3), jnp.logical_and(first, px < 3),
        ).start())

    gi_copies = []

    def backward(h):
        acc = jnp.dot(wg[...], patches(gb, h), preferred_element_type=F32)
        total = shift_lanes(acc[0:128], -1) + acc[128:256] + shift_lanes(acc[256:384], 1)
        gout[h] = total.astype(BF16)

    def send_rows(first, count):
        for k in range(1, 8):
            to = pl.ds(pl.multiple_of(16 * chan_peer(k), 16), 16)
            gi_copies.append(Copy(
                gout.at[pl.ds(first, count), to, :], back.at[pl.ds(4 * r + first, count)],
                gi_s, gi_r, {"chan": chan_peer(k)},
            ).start())
        back[pl.ds(4 * r + first, count)] = gout[first : first + count, mine, :]

    def finish_rows():
        drain(gb.at[1:5, :, 640:768], gh_r.at[6], has_hi)
        drain(gb.at[1:5, :, 0:128], gh_r.at[7], has_lo)
        backward(1)
        backward(2)
        send_rows(1, 2)
        for sent in row_rims:
            for copy in sent:
                copy.wait_recv()
        backward(0)
        backward(3)

    late = jnp.logical_or(g == 7, g == 8)
    pl.when(jnp.logical_not(late))(finish_rows)

    total = pair_sum(3)
    drain(xbuf, b_r)
    for j in range(3):
        total = total + xbuf[j].astype(F32)
    for slot in range(3):
        yb[slot] = total[slot].T.astype(BF16)
    yb[3] = jnp.zeros((128, 128), BF16)
    for copy in b9_copies:
        copy.wait_recv()

    @pl.when(jnp.logical_and(first, px < 3))
    def _():
        total9 = gw9[lax.min(px, 2)]
        for j in range(3):
            total9 = total9 + xbuf9[j].astype(F32)
        yb[3] = total9.T.astype(BF16)

    y_copies = []
    for dz in range(2):
        for k in range(8):
            if dz or k:
                z, to = lax.rem(pz + dz, 2), chan_peer(k)
                y_copies.append(Copy(
                    yb.at[:, pl.ds(pl.multiple_of(16 * to, 16), 16), :], ybuf.at[8 * pz + c],
                    y_s, y_r, {"space": 8 * z + 2 * px + core, "chan": to},
                ).start())
    ybuf[8 * pz + c] = yb[:, mine, :]
    pl.when(late)(finish_rows)
    send_rows(0, 1)
    send_rows(3, 1)
    drain(ybuf.at[0:15], y_r)
    total = ybuf[0].astype(F32)
    for n in range(1, 16):
        total = total + ybuf[n].astype(F32)
    piece = gwf.at[4 * core + px]
    piece[...] = total.astype(BF16)
    d_copies = [
        Copy(piece, piece, d_s, d_r, {"space": half_peer(k)}).start()
        for k in range(1, 8)
    ]
    drain(back.at[0:28], gi_r)
    for d in range(4):
        for h in range(32):
            wide[24 * h : 24 * h + 16, :] = back[h, :, 128 * d : 128 * d + 128].astype(F32)

        def step(ch, _):
            gi_ref[ch, d] = wide[pl.ds(ch, 32, stride=24), :].astype(BF16)
            return 0

        lax.fori_loop(0, 16, step, 0)
    out = pltpu.make_async_copy(gi_ref, gi_hbm, io_sem.at[0])
    out.start()
    drain(fp.at[0:28], wy_s, some)
    drain(xb.at[:, 0:112, 128:640], x_s)
    drain(ct.at[:, 0:112, :], t_s)
    drain(wall.at[0:12], wx_s, some)
    drain(wall.at[0:16], wd_s, core == 0)
    drain(wall.at[0:12], wd_s, core == 1)
    drain(xb.at[:, :, 128:256], xh_s.at[0], has_lo)
    drain(xb.at[:, :, 512:640], xh_s.at[1], has_hi)
    drain(gb.at[1:5, :, 128:256], gh_s.at[6], has_lo)
    drain(gb.at[1:5, :, 512:640], gh_s.at[7], has_hi)
    drain(back.at[0:28], gi_s)
    drain(gwb.at[0:4], a_s)
    drain(sb, b_s)
    drain(ybuf.at[0:15], y_s)
    for copy in row_rims[0] + row_rims[1] + [a9_copy] + b9_copies:
        copy.wait_send()
    drain(gwf.at[0:7], d_r)
    for tap in range(27):
        n, slot = (tap // 3, tap % 3) if tap < 24 else (tap - 24, 3)
        gw_ref[tap] = gwf[n, slot].astype(F32) * scale
    out_w = pltpu.make_async_copy(gw_ref, gw_hbm, io_sem.at[1])
    out_w.start()

    drain(gwf.at[0:7], d_s)
    out.wait()
    out_w.wait()


def hand_over(gi_in, gw_in, gi_out, gw_out, gi, gw, sems):
    pieces = [(gi_in.at[pl.ds(4 * n, 4)], gi.at[pl.ds(4 * n, 4)], gi_out.at[pl.ds(4 * n, 4)]) for n in range(4)]
    pieces.append((gw_in, gw, gw_out))
    loads = [pltpu.make_async_copy(src, mid, sems.at[0, n]) for n, (src, mid, _) in enumerate(pieces)]
    stores = [pltpu.make_async_copy(mid, dst, sems.at[1, n]) for n, (_, mid, dst) in enumerate(pieces)]
    for load in loads:
        load.start()
    for load, store in zip(loads, stores):
        load.wait()
        store.start()
    for store in stores:
        store.wait()


def body(inputs, filters, cotangent):
    cells = inputs.shape[1] * lax.axis_size("space") * inputs.shape[2] * inputs.shape[3]
    scale = 1.0 / math.sqrt(cells)
    sems = [0, 7, 0, 0, 0, 0, 0, 3, 0, 0, 2, 2, 8, 8, 0, 0, 0, 4, 0, 0, 0, 0, 3, 3, 0, 0, 0, 0, 3]
    scratch = [
        (inputs.shape, BF16),
        (filters.shape, BF16),
        (inputs.shape, BF16),
        (inputs.shape, BF16),
        (filters.shape, F32),
        ((PITCH * 16, 128), F32),
        ((34, 16, 512), BF16),
        ((32, 16, 512), BF16),
        ((32, 16, 128), BF16),
        ((6, 128, 768), BF16),
        ((4, 128, 512), BF16),
        ((32, 128, 128), BF16),
        ((384, 1152), BF16),
        ((384, 1152), BF16),
        ((4, 128, 512), F32),
        ((6, 768, 128), BF16),
        ((6, 128, 768), BF16),
        ((4, 384, 512), BF16),
        ((8, 3, 128, 128), F32),
        ((8, 3, 128, 128), BF16),
        ((4, 3, 128, 128), BF16),
        ((3, 3, 128, 128), BF16),
        ((3, 3, 128, 128), BF16),
        ((3, 128, 128), F32),
        ((3, 128, 128), BF16),
        ((3, 128, 128), BF16),
        ((3, 128, 128), BF16),
        ((3, 128, 128), BF16),
        ((4, 128, 128), BF16),
        ((16, 4, 16, 128), BF16),
        ((8, 4, 16, 128), BF16),
        ((4, 128, 512), BF16),
        ((32, 16, 512), BF16),
    ]
    hbm = pl.BlockSpec(memory_space=pl.ANY)
    grads = pl.pallas_call(
        lambda *refs: kernel(scale, *refs),
        out_shape=(
            jax.ShapeDtypeStruct(inputs.shape, BF16),
            jax.ShapeDtypeStruct(filters.shape, F32),
        ),
        in_specs=[hbm] * 3,
        out_specs=(hbm, hbm),
        scratch_shapes=[pltpu.VMEM(s, t) for s, t in scratch]
        + [pltpu.SemaphoreType.DMA((n,) if n else ()) for n in sems],
        compiler_params=pltpu.CompilerParams(
            collective_id=0, has_side_effects=True, vmem_limit_bytes=60 * 2**20
        ),
        name="conv_backward",
    )(inputs, filters, cotangent)
    return pl.pallas_call(
        hand_over,
        out_shape=tuple(jax.ShapeDtypeStruct(a.shape, a.dtype) for a in grads),
        in_specs=[hbm] * 2,
        out_specs=(hbm, hbm),
        scratch_shapes=[pltpu.VMEM(a.shape, a.dtype) for a in grads]
        + [pltpu.SemaphoreType.DMA((2, 5))],
        name="hand_over",
    )(*grads)


def solution(mesh):
    placed = (P("chan", "space", None, None), P(None, "chan", None), P("chan", "space", None, None))
    return jax.shard_map(
        body,
        mesh=mesh,
        in_specs=placed,
        out_specs=(P("chan", "space", None, None), P(None, "chan", None)),
        check_vma=False,
    )
```

```python
import math

import jax
import jax.numpy as jnp
from jax import lax
from jax.experimental import pallas as pl
from jax.experimental.pallas import tpu as pltpu
from jax.sharding import PartitionSpec as P

MESH = pl.DeviceIdType.MESH
BF16 = jnp.bfloat16
F32 = jnp.float32
PITCH = 136
STEPS = (2, 1, 3, 0)


def row_block(c):
    y = lax.div(c, 2)
    z = lax.rem(c, 2)
    q = lax.rem(y, 2)
    return 2 * y + z + q - 2 * z * q


class Copy:
    def __init__(self, src, dst, send_sem, recv_sem, where, sends=None, gets=None):
        self.copy = pltpu.make_async_remote_copy(
            src_ref=src, dst_ref=dst, send_sem=send_sem, recv_sem=recv_sem,
            device_id=where, device_id_type=MESH,
        )
        self.sends, self.gets = sends, gets

    def start(self):
        self.copy.start() if self.sends is None else pl.when(self.sends)(self.copy.start)
        return self

    def wait_recv(self):
        self.copy.wait_recv() if self.gets is None else pl.when(self.gets)(self.copy.wait_recv)

    def wait_send(self):
        self.copy.wait_send() if self.sends is None else pl.when(self.sends)(self.copy.wait_send)


def drain(like, sem, when=None):
    wait = pltpu.make_async_copy(like, like, sem).wait
    wait() if when is None else pl.when(when)(wait)


def shift_lanes(block, by):
    lane = lax.broadcasted_iota(jnp.int32, (block.shape[0], 128), 1)
    edge = 0 if by == 1 else 127
    pieces = []
    for d in range(block.shape[1] // 128):
        rolled = pltpu.roll(block[:, 128 * d : 128 * d + 128], by % 128, 1)
        pieces.append(jnp.where(lane == edge, 0.0, rolled))
    return jnp.concatenate(pieces, axis=1)


def kernel(
    scale, x_hbm, f_hbm, t_hbm, gi_hbm, gw_hbm,
    x_ref, f_ref, t_ref, gi_ref, gw_ref, wide, xt, tt, fp, xb, ct, wall, wg, wf, pre, xtt, gb, gs, gw, gwb, abuf, sb, xbuf,
    gw9, gwb9, abuf9, sb9, xbuf9, yb, ybuf, gwf,
    gout, back,
    x_s, x_r, t_s, t_r, wy_s, wy_r, wx_s, wx_r, wd_s, wd_r, xh_s, xh_r, gh_s, gh_r, gi_s, gi_r,
    a_s, a_r, a9_s, a9_r, b_s, b_r, b9_s, b9_r, y_s, y_r, d_s, d_r, io_sem,
):
    c = lax.axis_index("chan")
    g = lax.axis_index("space")
    r = row_block(c)
    core = lax.rem(g, 2)
    px = lax.rem(lax.div(g, 2), 4)
    pz = lax.div(g, 8)
    sibling = g + 1 - 2 * core
    mine = pl.ds(pl.multiple_of(16 * c, 16), 16)
    has_lo, has_hi = g > 0, g < 15
    has_up, has_down = r > 0, r < 7

    def chan_peer(k):
        return lax.rem(c + k, 8)

    def x_peer(k):
        return 8 * pz + 2 * lax.rem(px + k, 4) + core

    def half_peer(k):
        return 8 * pz + lax.rem(2 * px + core + k, 8)

    barrier = pltpu.get_barrier_semaphore()
    for k in range(1, 8):
        pl.semaphore_signal(barrier, inc=1, device_id={"chan": chan_peer(k)}, device_id_type=MESH)
    for k in range(1, 8):
        pl.semaphore_signal(barrier, inc=1, device_id={"space": half_peer(k)}, device_id_type=MESH)
    for k in range(8):
        pl.semaphore_signal(
            barrier, inc=1, device_id={"space": lax.rem(g + 8, 16), "chan": chan_peer(k)},
            device_id_type=MESH,
        )
    for edge, dg in ((7, 1), (8, -1)):

        @pl.when(g == edge)
        def _():
            pl.semaphore_signal(barrier, inc=1, device_id={"space": g + dg}, device_id_type=MESH)

    for dg, has_g in ((-1, has_lo), (1, has_hi)):
        for dr, has_r in ((-1, has_up), (1, has_down)):

            @pl.when(jnp.logical_and(has_g, has_r))
            def _():
                pl.semaphore_signal(
                    barrier, inc=1,
                    device_id={"space": g + dg, "chan": row_block(r + dr)}, device_id_type=MESH,
                )

    loads = [
        pltpu.make_async_copy(src, dst, io_sem.at[n])
        for n, (src, dst) in enumerate(((x_hbm, x_ref), (f_hbm, f_ref), (t_hbm, t_ref)))
    ]
    for load in loads:
        load.start()

    xt[0] = jnp.zeros((16, 512), BF16)
    xt[33] = jnp.zeros((16, 512), BF16)

    @pl.when(g == 0)
    def _():
        xb[:, :, 0:128] = jnp.zeros((6, 128, 128), BF16)
        gb[:, :, 0:128] = jnp.zeros((6, 128, 128), BF16)

    @pl.when(g == 15)
    def _():
        xb[:, :, 640:768] = jnp.zeros((6, 128, 128), BF16)
        gb[:, :, 640:768] = jnp.zeros((6, 128, 128), BF16)

    @pl.when(r == 0)
    def _():
        gb[0] = jnp.zeros((128, 768), BF16)

    @pl.when(r == 7)
    def _():
        gb[5] = jnp.zeros((128, 768), BF16)


    def to_rows(src, dst, first):
        for ch in range(16):
            wide[PITCH * ch : PITCH * ch + 128, :] = src[ch].reshape(128, 128).astype(F32)

        def step(h, _):
            for d in range(4):
                rows = wide[pl.ds(32 * d + h, 16, stride=PITCH), :]
                dst[first + h, :, 128 * d : 128 * d + 128] = rows.astype(BF16)
            return 0

        lax.fori_loop(0, 32, step, 0)

    loads[0].wait()
    to_rows(x_ref, xt, 1)
    sides_g = has_lo.astype(jnp.int32) + has_hi.astype(jnp.int32)
    sides_r = has_up.astype(jnp.int32) + has_down.astype(jnp.int32)
    middle = (g == 7).astype(jnp.int32) + (g == 8).astype(jnp.int32)
    loads[1].wait()
    fp[0:27] = f_ref[...]
    fp[27:32] = jnp.zeros((5, 16, 128), BF16)
    pl.semaphore_wait(barrier, 22 + middle + sides_g * sides_r)

    part = 4 * (4 * core + px)
    some = part < 28
    wy_copies = [
        Copy(
            fp.at[pl.ds(part, 4)], wall.at[pl.ds(part, 4), mine, :],
            wy_s, wy_r, {"chan": chan_peer(k)}, some, some,
        ).start()
        for k in range(1, 8)
    ]
    wall[pl.ds(part, 4), mine, :] = fp[pl.ds(part, 4)]
    x_copies = [
        Copy(
            xt.at[pl.ds(4 * row_block(chan_peer(k)), 6)], xb.at[:, mine, 128:640],
            x_s, x_r.at[k - 1], {"chan": chan_peer(k)},
        ).start()
        for k in range(1, 8)
    ]
    xb[:, mine, 128:640] = xt[pl.ds(4 * r, 6)]
    loads[2].wait()
    to_rows(t_ref, tt, 0)
    t_copies = [
        Copy(
            tt.at[pl.ds(4 * row_block(chan_peer(k)), 4)], ct.at[:, mine, :],
            t_s, t_r, {"chan": chan_peer(k)},
        ).start()
        for k in range(1, 8)
    ]
    ct[:, mine, :] = tt[pl.ds(4 * r, 4)]
    drain(fp.at[0:28], wy_r, some)
    wx_copies = [
        Copy(
            wall.at[pl.ds(part, 4)], wall.at[pl.ds(part, 4)],
            wx_s, wx_r.at[k - 1], {"space": x_peer(k)},
            some, core + lax.rem(px + 4 - k, 4) < 4,
        ).start()
        for k in range(1, 4)
    ]

    wd_copies = []

    def pass_filters(k):
        owner = lax.rem(px + 4 - k, 4)
        piece = wall.at[pl.ds(4 * (4 * core + owner), 4)]
        wd_copies.append(Copy(
            piece, piece, wd_s, wd_r, {"space": sibling},
            core + owner < 4, 1 - core + owner < 4,
        ).start())

    pass_filters(0)

    h_copies = []

    def pass_rims(k):
        rows = pl.ds(pl.multiple_of(16 * lax.rem(c + 8 - k, 8), 16), 16)
        for n, at, to, dg in ((0, 128, 640, -1), (1, 512, 0, 1)):
            has_g, from_g = (has_lo, has_hi) if dg < 0 else (has_hi, has_lo)
            h_copies.append(Copy(
                xb.at[:, rows, at : at + 128], xb.at[:, rows, to : to + 128],
                xh_s.at[n], xh_r.at[n], {"space": g + dg}, has_g, from_g,
            ).start())

    pass_rims(0)
    for k in range(1, 6):
        x_copies[k - 1].wait_recv()
        pass_rims(k)
    for k in range(1, 4):
        wx_copies[k - 1].wait_recv()
        pass_filters(k)
    for k in range(6, 8):
        x_copies[k - 1].wait_recv()
        pass_rims(k)
    drain(wall.at[0:12], wd_r, core == 0)
    drain(wall.at[0:16], wd_r, core == 1)
    for tap in range(27):
        a, b, cc = tap // 9, tap // 3 % 3, tap % 3
        block = wall[tap]
        rows = slice(128 * cc, 128 * cc + 128)
        wg[rows, 128 * (8 - 3 * a - b) : 128 * (9 - 3 * a - b)] = block
        wf[rows, 128 * (3 * a + b) : 128 * (3 * a + b + 1)] = block.T
    drain(xb.at[:, :, 640:768], xh_r.at[0], has_hi)
    drain(xb.at[:, :, 0:128], xh_r.at[1], has_lo)

    def patches(src, h):
        rows = [src[h + b, :, 128 * a : 128 * a + 512] for a in range(3) for b in range(3)]
        return jnp.concatenate(rows, axis=0)

    def forward(h, _):
        acc = jnp.dot(wf[...], patches(xb, h), preferred_element_type=F32)
        pre[h] = shift_lanes(acc[0:128], 1) + acc[128:256] + shift_lanes(acc[256:384], -1)
        for n in range(9):
            row, plane = lax.div(9 * h + n, 6), lax.rem(9 * h + n, 6)
            at = pl.ds(pl.multiple_of(128 * plane, 128), 128)
            xtt[row, at, :] = xb[row, :, at].T
        return 0

    lax.fori_loop(0, 4, forward, 0)
    drain(ct.at[:, 0:112, :], t_r)

    up, down = row_block(lax.max(r - 1, 0)), row_block(lax.min(r + 1, 7))
    row_rims, plane_rims = [], []

    def send_rims(row, to_row, has_r, from_r, to):
        n = 3 * len(row_rims)
        sent = [Copy(
            gb.at[row, :, 128:640], gb.at[to_row, :, 128:640], gh_s.at[n], gh_r.at[n],
            {"chan": to}, has_r, from_r,
        ).start()]
        for m, plane, to_plane, dg in ((1, 128, 640, -1), (2, 512, 0, 1)):
            has_g, from_g = (has_lo, has_hi) if dg < 0 else (has_hi, has_lo)
            sent.append(Copy(
                gb.at[row, :, plane : plane + 128], gb.at[to_row, :, to_plane : to_plane + 128],
                gh_s.at[n + m], gh_r.at[n + m], {"space": g + dg, "chan": to},
                jnp.logical_and(has_g, has_r), jnp.logical_and(from_g, from_r),
            ).start())
        row_rims.append(sent)

    for h in (0, 3, 1, 2):
        p = pre[h]
        sigma = 1.0 / (1.0 + jnp.exp(-p))
        grad = ct[h].astype(F32) * sigma * (1.0 + p * (1.0 - sigma))
        gb[h + 1, :, 128:640] = grad.astype(BF16)
        for n, at, to, dg in ((6, 128, 640, -1), (7, 512, 0, 1)):
            has_g, from_g = (has_lo, has_hi) if dg < 0 else (has_hi, has_lo)
            plane_rims.append(Copy(
                gb.at[h + 1, :, at : at + 128], gb.at[h + 1, :, to : to + 128],
                gh_s.at[n], gh_r.at[n], {"space": g + dg}, has_g, from_g,
            ).start())
        if h == 0:
            send_rims(1, 5, has_up, has_down, up)
        if h == 3:
            send_rims(4, 0, has_down, has_up, down)
        gs[h, 0:128, :] = shift_lanes(grad, -1).astype(BF16)
        gs[h, 128:256, :] = grad.astype(BF16)
        gs[h, 256:384, :] = shift_lanes(grad, 1).astype(BF16)

    grads = jnp.concatenate([gs[h] for h in range(4)], axis=1)

    def product(*offsets):
        sides = []
        for ab in offsets:
            lanes = pl.ds(pl.multiple_of(128 * lax.div(ab, 3), 128), 512)
            rows = [xtt[h + lax.rem(ab, 3), lanes, :] for h in range(4)]
            sides.append(jnp.concatenate(rows, axis=0))
        side = sides[0] if len(sides) == 1 else jnp.concatenate(sides, axis=1)
        return jnp.dot(grads, side, preferred_element_type=F32)

    a_copies, b_copies = [], []
    first = core == 0

    def pair_sum(j):
        a_copies[j].wait_recv()
        q = lax.rem(px + STEPS[j], 4)
        total = gw[4 * core + q] + abuf[j].astype(F32)
        if STEPS[j] == 0:
            return total
        sb[j] = total.astype(BF16)
        b_copies.append(Copy(
            sb.at[j], xbuf.at[j], b_s, b_r, {"space": x_peer(STEPS[j])}
        ).start())

    for j in range(4):
        q = lax.rem(px + STEPS[j], 4)
        prod = product(q, q + 4)
        for cc in range(3):
            for n in range(2):
                block = prod[128 * cc : 128 * cc + 128, 128 * n : 128 * n + 128]
                gw[4 * n + q, cc] = block
                gwb[4 * n + q, cc] = block.astype(BF16)
        a_copies.append(Copy(
            gwb.at[4 * (1 - core) + q], abuf.at[j], a_s, a_r.at[j], {"space": sibling}
        ).start())
        if j == 1:
            ninth = product(jnp.int32(8))
            for n in range(3):
                gw9[n] = ninth[128 * n : 128 * n + 128]
                gwb9[n] = ninth[128 * n : 128 * n + 128].astype(BF16)
            a9_copy = Copy(
                gwb9, abuf9, a9_s, a9_r, {"space": sibling}, core == 1, first
            ).start()
        if j:
            pair_sum(j - 1)
    a9_copy.wait_recv()

    @pl.when(first)
    def _():
        gw9[...] = gw9[...] + abuf9[...].astype(F32)
        sb9[...] = gw9[...].astype(BF16)

    b9_copies = []
    for k in range(1, 4):
        q = lax.rem(px + k, 4)
        b9_copies.append(Copy(
            sb9.at[lax.min(q, 2)], xbuf9.at[k - 1], b9_s.at[k - 1], b9_r.at[k - 1],
            {"space": x_peer(k)}, jnp.logical_and(first, q < 3), jnp.logical_and(first, px < 3),
        ).start())

    gi_copies = []

    def backward(h):
        acc = jnp.dot(wg[...], patches(gb, h), preferred_element_type=F32)
        total = shift_lanes(acc[0:128], -1) + acc[128:256] + shift_lanes(acc[256:384], 1)
        gout[h] = total.astype(BF16)

    def send_rows(first, count):
        for k in range(1, 8):
            to = pl.ds(pl.multiple_of(16 * chan_peer(k), 16), 16)
            gi_copies.append(Copy(
                gout.at[pl.ds(first, count), to, :], back.at[pl.ds(4 * r + first, count)],
                gi_s, gi_r, {"chan": chan_peer(k)},
            ).start())
        back[pl.ds(4 * r + first, count)] = gout[first : first + count, mine, :]

    def finish_rows():
        drain(gb.at[1:5, :, 640:768], gh_r.at[6], has_hi)
        drain(gb.at[1:5, :, 0:128], gh_r.at[7], has_lo)
        backward(1)
        backward(2)
        send_rows(1, 2)
        for sent in row_rims:
            for copy in sent:
                copy.wait_recv()
        backward(0)
        backward(3)

    late = g == 8
    pl.when(jnp.logical_not(late))(finish_rows)

    total = pair_sum(3)
    drain(xbuf, b_r)
    for j in range(3):
        total = total + xbuf[j].astype(F32)
    for slot in range(3):
        yb[slot] = total[slot].T.astype(BF16)
    yb[3] = jnp.zeros((128, 128), BF16)
    for copy in b9_copies:
        copy.wait_recv()

    @pl.when(jnp.logical_and(first, px < 3))
    def _():
        total9 = gw9[lax.min(px, 2)]
        for j in range(3):
            total9 = total9 + xbuf9[j].astype(F32)
        yb[3] = total9.T.astype(BF16)

    y_copies = []
    for dz in range(2):
        for k in range(8):
            if dz or k:
                z, to = lax.rem(pz + dz, 2), chan_peer(k)
                y_copies.append(Copy(
                    yb.at[:, pl.ds(pl.multiple_of(16 * to, 16), 16), :], ybuf.at[8 * pz + c],
                    y_s, y_r, {"space": 8 * z + 2 * px + core, "chan": to},
                ).start())
    ybuf[8 * pz + c] = yb[:, mine, :]
    pl.when(late)(finish_rows)
    send_rows(0, 1)
    send_rows(3, 1)
    drain(ybuf.at[0:15], y_r)
    total = ybuf[0].astype(F32)
    for n in range(1, 16):
        total = total + ybuf[n].astype(F32)
    piece = gwf.at[4 * core + px]
    piece[...] = total.astype(BF16)
    d_copies = [
        Copy(piece, piece, d_s, d_r, {"space": half_peer(k)}).start()
        for k in range(1, 8)
    ]
    drain(back.at[0:28], gi_r)
    for d in range(4):
        for h in range(32):
            wide[24 * h : 24 * h + 16, :] = back[h, :, 128 * d : 128 * d + 128].astype(F32)

        def step(ch, _):
            gi_ref[ch, d] = wide[pl.ds(ch, 32, stride=24), :].astype(BF16)
            return 0

        lax.fori_loop(0, 16, step, 0)
    out = pltpu.make_async_copy(gi_ref, gi_hbm, io_sem.at[0])
    out.start()
    drain(fp.at[0:28], wy_s, some)
    drain(xb.at[:, 0:112, 128:640], x_s)
    drain(ct.at[:, 0:112, :], t_s)
    drain(wall.at[0:12], wx_s, some)
    drain(wall.at[0:16], wd_s, core == 0)
    drain(wall.at[0:12], wd_s, core == 1)
    drain(xb.at[:, :, 128:256], xh_s.at[0], has_lo)
    drain(xb.at[:, :, 512:640], xh_s.at[1], has_hi)
    drain(gb.at[1:5, :, 128:256], gh_s.at[6], has_lo)
    drain(gb.at[1:5, :, 512:640], gh_s.at[7], has_hi)
    drain(back.at[0:28], gi_s)
    drain(gwb.at[0:4], a_s)
    drain(sb, b_s)
    drain(ybuf.at[0:15], y_s)
    for copy in row_rims[0] + row_rims[1] + [a9_copy] + b9_copies:
        copy.wait_send()
    drain(gwf.at[0:7], d_r)
    for tap in range(27):
        n, slot = (tap // 3, tap % 3) if tap < 24 else (tap - 24, 3)
        gw_ref[tap] = gwf[n, slot].astype(F32) * scale
    out_w = pltpu.make_async_copy(gw_ref, gw_hbm, io_sem.at[1])
    out_w.start()

    drain(gwf.at[0:7], d_s)
    out.wait()
    out_w.wait()


def hand_over(gi_in, gw_in, gi_out, gw_out, gi, gw, sems):
    pieces = [(gi_in.at[pl.ds(4 * n, 4)], gi.at[pl.ds(4 * n, 4)], gi_out.at[pl.ds(4 * n, 4)]) for n in range(4)]
    pieces.append((gw_in, gw, gw_out))
    loads = [pltpu.make_async_copy(src, mid, sems.at[0, n]) for n, (src, mid, _) in enumerate(pieces)]
    stores = [pltpu.make_async_copy(mid, dst, sems.at[1, n]) for n, (_, mid, dst) in enumerate(pieces)]
    for load in loads:
        load.start()
    for load, store in zip(loads, stores):
        load.wait()
        store.start()
    for store in stores:
        store.wait()


def body(inputs, filters, cotangent):
    cells = inputs.shape[1] * lax.axis_size("space") * inputs.shape[2] * inputs.shape[3]
    scale = 1.0 / math.sqrt(cells)
    sems = [0, 7, 0, 0, 0, 0, 0, 3, 0, 0, 2, 2, 8, 8, 0, 0, 0, 4, 0, 0, 0, 0, 3, 3, 0, 0, 0, 0, 3]
    scratch = [
        (inputs.shape, BF16),
        (filters.shape, BF16),
        (inputs.shape, BF16),
        (inputs.shape, BF16),
        (filters.shape, F32),
        ((PITCH * 17, 128), F32),
        ((34, 16, 512), BF16),
        ((32, 16, 512), BF16),
        ((32, 16, 128), BF16),
        ((6, 128, 768), BF16),
        ((4, 128, 512), BF16),
        ((32, 128, 128), BF16),
        ((384, 1152), BF16),
        ((384, 1152), BF16),
        ((4, 128, 512), F32),
        ((6, 768, 128), BF16),
        ((6, 128, 768), BF16),
        ((4, 384, 512), BF16),
        ((8, 3, 128, 128), F32),
        ((8, 3, 128, 128), BF16),
        ((4, 3, 128, 128), BF16),
        ((3, 3, 128, 128), BF16),
        ((3, 3, 128, 128), BF16),
        ((3, 128, 128), F32),
        ((3, 128, 128), BF16),
        ((3, 128, 128), BF16),
        ((3, 128, 128), BF16),
        ((3, 128, 128), BF16),
        ((4, 128, 128), BF16),
        ((16, 4, 16, 128), BF16),
        ((8, 4, 16, 128), BF16),
        ((4, 128, 512), BF16),
        ((32, 16, 512), BF16),
    ]
    hbm = pl.BlockSpec(memory_space=pl.ANY)
    grads = pl.pallas_call(
        lambda *refs: kernel(scale, *refs),
        out_shape=(
            jax.ShapeDtypeStruct(inputs.shape, BF16),
            jax.ShapeDtypeStruct(filters.shape, F32),
        ),
        in_specs=[hbm] * 3,
        out_specs=(hbm, hbm),
        scratch_shapes=[pltpu.VMEM(s, t) for s, t in scratch]
        + [pltpu.SemaphoreType.DMA((n,) if n else ()) for n in sems],
        compiler_params=pltpu.CompilerParams(
            collective_id=0, has_side_effects=True, vmem_limit_bytes=60 * 2**20
        ),
        name="conv_backward",
    )(inputs, filters, cotangent)
    return pl.pallas_call(
        hand_over,
        out_shape=tuple(jax.ShapeDtypeStruct(a.shape, a.dtype) for a in grads),
        in_specs=[hbm] * 2,
        out_specs=(hbm, hbm),
        scratch_shapes=[pltpu.VMEM(a.shape, a.dtype) for a in grads]
        + [pltpu.SemaphoreType.DMA((2, 5))],
        name="hand_over",
    )(*grads)


def solution(mesh):
    placed = (P("chan", "space", None, None), P(None, "chan", None), P("chan", "space", None, None))
    return jax.shard_map(
        body,
        mesh=mesh,
        in_specs=placed,
        out_specs=(P("chan", "space", None, None), P(None, "chan", None)),
        check_vma=False,
    )
```
